256 devices in a mesh: vert: 64 (over z, y, core), edge: 4 (over x).
Axes of the slice: x: 4, y: 4, z: 8, core: 2. Of those that a mesh axis runs over, the one named last changes fastest.
Arguments:
- features: float32 [131072, 256], P('vert'), may hold values from -6 to 6
- incidence: bfloat16 [4096, 128, 512], P('vert', None, 'edge'), may hold values from 0 to 1, as said below
- send_count: int32 [4096, 4], P('vert', 'edge'), may hold values from 0 to 1, as said below
- row_block: int32 [4096, 4], P('vert', 'edge'), may hold values from 0 to 15
- edge_block: int32 [4096, 4], P('vert', 'edge'), may hold values from 0 to 1
- edge_weight: float32 [128, 512], P('vert', 'edge'), may hold values from 0.25 to 4
- edge_degree: int32 [128, 512], P('vert', 'edge'), may hold values from 0 to 8192, as said below
- vertex_degree: int32 [131072], P('vert'), may hold values from 0 to 32768, as said below
Outputs:
- smoothed: float32 [131072, 256], P(('vert', 'edge'))
The draws below stay inside these ranges and needn't reach their ends.
Inputs may be any that keep to these rules, and one draw needn't show every extreme that they name: `incidence`: tile entries are 0 or 1. `send_count`: for each edge index one hyperedge block receives a live tile from every index of vert, in every draw. `edge_degree`: the column sums of H over live tiles; the most is reached in every draw. `vertex_degree`: the row sums of H over live tiles; the most is reached in every draw.
All inputs are finite; a program needn't handle non-finite values.
Results may differ from the reference program's by a relative error of at most 0.0049.
Values may be sent and summed in bfloat16 or wider, within the bound.
No kernel may reach another device: no remote copies, remote signals or barrier semaphores. Data moves between devices by JAX's collectives and lax.ppermute only.
A program may use at most 64 MiB of HBM per device.

```python
import math
import jax
import jax.numpy as jnp
from jax import lax

ROWS_DEV = 2048
F = 256
BLOCK = 128
HB_DEV = 2
PAPERS = 131072
N_VERT = 64
N_EDGE = 4


def hyper_plan(key):
    base = jax.random.fold_in(key, 11)
    keys = jax.random.split(base, 7)
    vert_total = N_VERT
    edge_total = N_EDGE
    block_count = ROWS_DEV // BLOCK
    shape = (vert_total, vert_total, edge_total)
    send_live = (jax.random.randint(keys[0], shape, 0, 4) == 0).astype(jnp.int32)
    row_pick = jax.random.randint(keys[1], shape, 0, block_count).astype(jnp.int32)
    edge_pick = jax.random.randint(keys[2], shape, 0, HB_DEV).astype(jnp.int32)
    giant_owner = jax.random.randint(keys[3], (edge_total,), 0, vert_total)
    giant_block = jax.random.randint(keys[4], (edge_total,), 0, HB_DEV).astype(jnp.int32)
    is_giant = jnp.arange(vert_total)[None, :, None] == giant_owner[None, None, :]
    first_source = jnp.arange(vert_total)[:, None, None] == 0
    send_live = jnp.where(is_giant, 1, send_live).astype(jnp.int32)
    send_live = jnp.where(first_source, 1, send_live).astype(jnp.int32)
    row_pick = jnp.where(first_source, 0, row_pick).astype(jnp.int32)
    edge_pick = jnp.where(is_giant, giant_block[None, None, :], edge_pick).astype(jnp.int32)
    active = (jax.random.randint(keys[5], (vert_total, block_count, BLOCK), 0, 32) > 0).astype(jnp.int32)
    tile_bits = (jax.random.randint(keys[6], (vert_total, vert_total, BLOCK, edge_total, BLOCK), 0, 50) == 0).astype(jnp.int32)
    diagonal = (jnp.arange(BLOCK)[:, None] == jnp.arange(BLOCK)[None, :]).astype(jnp.int32)
    tile_bits = jnp.maximum(tile_bits, diagonal[None, None, :, None, :])
    row_active = active[jnp.arange(vert_total)[:, None, None], row_pick]
    tile_bits = tile_bits * jnp.transpose(row_active, (0, 1, 3, 2))[:, :, :, :, None]
    column_first = (jnp.arange(BLOCK) == 0)[None, None, None, None, :]
    giant_column = jnp.logical_and(jnp.broadcast_to(is_giant, shape)[:, :, None, :, None], column_first)
    tile_bits = jnp.maximum(tile_bits, giant_column.astype(jnp.int32))
    row_first = (jnp.arange(BLOCK) == 0)[None, None, :, None, None]
    full_row = jnp.logical_and(first_source[:, :, :, None, None], row_first)
    tile_bits = jnp.maximum(tile_bits, full_row.astype(jnp.int32))
    return (send_live, row_pick, edge_pick, tile_bits)


def draw_incidence(key, part):
    send_live, row_pick, edge_pick, tile_bits = hyper_plan(key)
    flat = tile_bits.reshape(N_VERT * N_VERT, BLOCK, N_EDGE * BLOCK)
    return flat.astype(jnp.float32).astype(jnp.bfloat16)


def draw_send_count(key, part):
    send_live, row_pick, edge_pick, tile_bits = hyper_plan(key)
    return send_live.reshape(N_VERT * N_VERT, N_EDGE)


def draw_row_block(key, part):
    send_live, row_pick, edge_pick, tile_bits = hyper_plan(key)
    return row_pick.reshape(N_VERT * N_VERT, N_EDGE)


def draw_edge_block(key, part):
    send_live, row_pick, edge_pick, tile_bits = hyper_plan(key)
    return edge_pick.reshape(N_VERT * N_VERT, N_EDGE)


def draw_edge_degree(key, part):
    send_live, row_pick, edge_pick, tile_bits = hyper_plan(key)
    live_bits = tile_bits * send_live[:, :, None, :, None]
    column_sums = jnp.sum(live_bits, axis=2)
    choose = (edge_pick[:, :, :, None] == jnp.arange(HB_DEV)[None, None, None, :]).astype(jnp.int32)
    degree = jnp.einsum('vdeh,vdeq->dheq', choose, column_sums)
    return degree.reshape(N_VERT * HB_DEV, N_EDGE * BLOCK).astype(jnp.int32)


def draw_vertex_degree(key, part):
    send_live, row_pick, edge_pick, tile_bits = hyper_plan(key)
    live_bits = tile_bits * send_live[:, :, None, :, None]
    row_sums = jnp.sum(live_bits, axis=4)
    choose = (row_pick[:, :, :, None] == jnp.arange(ROWS_DEV // BLOCK)[None, None, None, :]).astype(jnp.int32)
    degree = jnp.einsum('vdeb,vdpe->vbp', choose, row_sums)
    return degree.reshape(N_VERT * ROWS_DEV).astype(jnp.int32)


def levels(rng, shape, pieces, least, top_value):
    factor_of = 1.0
    for dim, parts in pieces:
        steps = jax.random.uniform(jax.random.fold_in(jax.random.fold_in(rng, 6), dim), (parts,), jnp.float32, least / len(pieces), top_value / len(pieces))
        factor_of = factor_of * jnp.repeat(jnp.exp(steps), shape[dim] // parts).reshape((-1,) + (1,) * (len(shape) - 1 - dim))
    return factor_of


def centred(rng, shape, scale, bound, cuts=(), dtype=jnp.bfloat16):
    level = levels(rng, shape, cuts, -0.22, 0.18) if cuts else 1.0
    drawn = jax.random.normal(rng, shape, jnp.float32) * scale * level
    return jnp.minimum(jnp.maximum(drawn, -bound), bound).astype(dtype)


def setup_inputs(seed: int = 0) -> dict:
    splits = jax.random.split(jax.random.key(seed), 9)
    return {
        "features": centred(splits[0], (PAPERS, F), 1.0, 6.0, ((0, 64),), jnp.float32),
        "incidence": draw_incidence(jax.random.fold_in(splits[8], 71), 0),
        "send_count": draw_send_count(jax.random.fold_in(splits[8], 71), 0),
        "row_block": draw_row_block(jax.random.fold_in(splits[8], 71), 0),
        "edge_block": draw_edge_block(jax.random.fold_in(splits[8], 71), 0),
        "edge_weight": jnp.clip(jnp.exp(math.log(4.0) - 2.7725887 * jax.random.uniform(splits[5], (N_VERT * HB_DEV, N_EDGE * BLOCK), jnp.float32) ** levels(splits[5], (N_VERT * HB_DEV, N_EDGE * BLOCK), ((0, 64), (1, 4)), -0.2, 0.2)), 0.25, 4.0),
        "edge_degree": draw_edge_degree(jax.random.fold_in(splits[8], 71), 0),
        "vertex_degree": draw_vertex_degree(jax.random.fold_in(splits[8], 71), 0),
    }


def reference(features, incidence, send_count, row_block, edge_block, edge_weight, edge_degree, vertex_degree):
    vert_total = N_VERT
    edge_total = N_EDGE
    block_count = ROWS_DEV // BLOCK
    tile_set = incidence.reshape(vert_total, vert_total, BLOCK, edge_total, BLOCK)
    live_slot = send_count.reshape(vert_total, vert_total, edge_total).astype(jnp.float32)
    row_index = row_block.reshape(vert_total, vert_total, edge_total)
    edge_index = edge_block.reshape(vert_total, vert_total, edge_total)
    row_scale = 1.0 / jnp.sqrt(jnp.maximum(vertex_degree, 1).astype(jnp.float32))
    row_scale = row_scale.reshape(vert_total, block_count, BLOCK, 1)
    hyper_scale = edge_weight / jnp.maximum(edge_degree, 1).astype(jnp.float32)
    hyper_scale = hyper_scale.reshape(vert_total, HB_DEV, edge_total, BLOCK, 1)
    owners = jnp.arange(vert_total)
    blocks = jnp.arange(block_count)
    hyper_ids = jnp.arange(HB_DEV)
    edge_ids = jnp.arange(edge_total)

    def apply_once(scaled_rows):

        def forward(total, source):
            tiles_here = tile_set[source].astype(jnp.float32)
            picked = scaled_rows[source][row_index[source]].astype(jnp.float32)
            partial_value = jnp.einsum('dpeq,depf->deqf', tiles_here, picked, precision=lax.Precision.HIGHEST)
            partial_value = (partial_value * live_slot[source][:, :, None, None]).astype(jnp.bfloat16).astype(jnp.float32)
            choose = (edge_index[source][:, :, None] == hyper_ids[None, None, :]).astype(jnp.float32)
            return (total + choose.transpose(0, 2, 1)[:, :, :, None, None] * partial_value[:, None], None)
        zero = jnp.zeros((vert_total, HB_DEV, edge_total, BLOCK, F), jnp.float32)
        summed, _ = lax.scan(forward, zero, owners)
        reply_all = (summed * hyper_scale).astype(jnp.bfloat16)

        def backward(source):
            reply = reply_all[owners[:, None], edge_index[source], edge_ids[None, :]].astype(jnp.float32)
            tiles_here = tile_set[source].astype(jnp.float32)
            spread = jnp.einsum('dpeq,deqf->dpef', tiles_here, reply, precision=lax.Precision.HIGHEST)
            choose = (row_index[source][None] == blocks[:, None, None]).astype(jnp.float32) * live_slot[source][None]
            return jnp.einsum('bde,dpef->bpf', choose, spread, precision=lax.Precision.HIGHEST)
        return lax.map(backward, owners)
    current = features.reshape(vert_total, block_count, BLOCK, F)
    for applied in range(2):
        scaled = (row_scale * current).astype(jnp.bfloat16)
        current = row_scale * apply_once(scaled)
    return current.reshape(vert_total * ROWS_DEV, F)
```

```python
import functools

import jax
import jax.numpy as jnp
from jax import lax
from jax.experimental import pallas as pl
from jax.experimental.pallas import tpu as pltpu
from jax.sharding import PartitionSpec as P

NZ, NY, NC, NX = 8, 4, 2, 4
T = 128
BF = jnp.bfloat16
F32 = jnp.float32


def moved(dz, dy, flip):
    pairs = []
    for z in range(NZ):
        for y in range(NY):
            for c in range(NC):
                here = (z * NY + y) * NC + c
                there = (((z + dz) % NZ) * NY + (y + dy) % NY) * NC + (c ^ flip)
                pairs.append((here, there))
    return pairs


def along_z(a, step):
    return lax.ppermute(a, "vert", moved(step, 0, 0))


def along_y(a, step):
    return lax.ppermute(a, "vert", moved(0, step, 0))


def to_sibling(a):
    return lax.ppermute(a, "vert", moved(0, 0, 1))


def along_x(a, step):
    return lax.ppermute(a, "edge", [(i, (i + step) % NX) for i in range(NX)])


def forward_body(info, code, pick, st, inc0, inc1, out):
    step = pl.program_id(0)
    z = info[0]
    y_to = info[1 + step]

    def one(dz, carry):
        z_to = lax.rem(z + dz, NZ)
        for c in range(NC):
            slot = (z_to * NY + y_to) * NC + c
            a0 = st[pick[slot]]
            a1 = st[pick[NZ * NY * NC + slot]]
            k0 = code[slot]
            k1 = code[NZ * NY * NC + slot]
            zero = jnp.zeros_like(a0)
            rows = [
                jnp.concatenate(
                    [jnp.where(k0 == b, a0, zero), jnp.where(k1 == b, a1, zero)], axis=1
                )
                for b in range(2)
            ]
            left = jnp.concatenate(rows, axis=0)
            right = jnp.concatenate([inc0[z_to, 0, c], inc1[z_to, 0, c]], axis=0)
            got = jnp.dot(left, right, preferred_element_type=F32).astype(out.dtype)
            out[0, dz, 2 * c] = got[:T]
            out[0, dz, 2 * c + 1] = got[T:]
        return carry

    lax.fori_loop(0, NZ, one, 0, unroll=2)


def forward(dys, dtype, z, y, code, pick, st, inc0, inc1):
    count = len(dys)
    info = jnp.stack([z] + [(y + dy) % NY for dy in dys]).astype(jnp.int32)
    tiles = pl.BlockSpec((NZ, 1, NC, T, T), lambda i, info, code, pick: (0, info[1 + i], 0, 0, 0))
    return pl.pallas_call(
        forward_body,
        out_shape=jax.ShapeDtypeStruct((count, NZ, 2 * NC, T, T), dtype),
        grid_spec=pltpu.PrefetchScalarGridSpec(
            num_scalar_prefetch=3,
            grid=(count,),
            in_specs=[
                pl.BlockSpec((2 * 16, T, T), lambda i, *_: (0, 0, 0)),
                tiles,
                tiles,
            ],
            out_specs=pl.BlockSpec((1, NZ, 2 * NC, T, T), lambda i, *_: (i, 0, 0, 0, 0)),
        ),
        name="tiles_forward",
    )(info, code, pick, st, inc0, inc1)


def backward_body(groups, first, info, code, pick, *refs):
    refs = list(refs)
    before = None if first else refs.pop(0)
    total = refs.pop()
    if first:
        total[...] = jnp.zeros_like(total)
    else:
        total[...] = before[...]
    z = info[0]
    for g, pieces in enumerate(groups):
        y_to = info[1 + g]
        inc0 = refs.pop(0)
        inc1 = refs.pop(0)
        for start, size in pieces:
            held = refs.pop(0)

            def one(i, carry, y_to=y_to, inc=(inc0, inc1), start=start, held=held):
                z_to = lax.rem(z + start + i, NZ)
                sums = []
                for c in range(NC):
                    slot = (z_to * NY + y_to) * NC + c
                    for s in range(2):
                        k = code[s * NZ * NY * NC + slot]
                        h = held[i, 2 * c + jnp.maximum(k, 0)]
                        h = jnp.where(k >= 0, h, jnp.zeros_like(h))
                        got = lax.dot_general(
                            h,
                            inc[s][z_to, 0, c],
                            (((1,), (1,)), ((), ())),
                            preferred_element_type=F32,
                        )
                        sums.append((pick[s * NZ * NY * NC + slot], got))
                for row, got in sums:
                    total[row] += got
                return carry

            lax.fori_loop(0, size, one, 0)


def backward(dys, pieces, before, z, y, code, pick, inc0, inc1, helds):
    info = jnp.stack([z] + [(y + dy) % NY for dy in dys]).astype(jnp.int32)
    first = before is None
    whole = pl.BlockSpec((2 * 16, T, T), lambda i, *_: (0, 0, 0))
    specs = [] if first else [whole]
    args = [] if first else [before]
    for g in range(len(dys)):
        for inc in (inc0, inc1):
            specs.append(
                pl.BlockSpec(
                    (NZ, 1, NC, T, T),
                    lambda i, info, code, pick, g=g: (0, info[1 + g], 0, 0, 0),
                )
            )
            args.append(inc)
        for held in helds[g]:
            specs.append(pl.BlockSpec(held.shape, lambda i, *_: (0, 0, 0, 0)))
            args.append(held)
    return pl.pallas_call(
        functools.partial(backward_body, pieces, first),
        out_shape=jax.ShapeDtypeStruct((2 * 16, T, T), F32),
        grid_spec=pltpu.PrefetchScalarGridSpec(
            num_scalar_prefetch=3,
            grid=(1,),
            in_specs=specs,
            out_specs=whole,
        ),
        input_output_aliases={} if first else {3: 0},
        name="tiles_backward",
    )(info, code, pick, *args)


def low(a, b, m):
    return jnp.concatenate([a[:m] + b.astype(F32), a[m:]], axis=0).astype(BF)


def high(a, b, m):
    return jnp.concatenate([a[:m], a[m:] + b.astype(F32)], axis=0).astype(BF)


def shards(
    features, incidence, send_count, row_block, edge_block, edge_weight, edge_degree, vertex_degree
):
    vert = lax.axis_index("vert")
    x = lax.axis_index("edge")
    z, y, c = vert // (NY * NC), (vert // NC) % NY, vert % NC
    slots = NZ * NY * NC
    rows = features.shape[0]
    blocks = rows // T
    per = blocks // NX

    row_scale = 1.0 / jnp.sqrt(jnp.maximum(vertex_degree, 1).astype(F32))
    hyper_scale = edge_weight / jnp.maximum(edge_degree, 1).astype(F32)
    mine = jnp.concatenate(
        [
            row_scale,
            hyper_scale.reshape(-1),
            send_count[:, 0].astype(F32),
            row_block[:, 0].astype(F32),
            edge_block[:, 0].astype(F32),
        ]
    )
    theirs = to_sibling(mine)
    both = jnp.stack([mine, theirs])
    at = rows + 2 * T
    live = both[:, at : at + slots] > 0.5
    row_of = jnp.round(both[:, at + slots : at + 2 * slots]).astype(jnp.int32)
    edge_of = jnp.round(both[:, at + 2 * slots : at + 3 * slots]).astype(jnp.int32)
    code = jnp.where(live, edge_of, -1).reshape(-1)
    side = jnp.arange(2, dtype=jnp.int32)[:, None]
    pick_first = (side * blocks + row_of).reshape(-1)
    pick_rel = ((((row_of // per) - x) % NX) * 2 * per + side * per + row_of % per).reshape(-1)
    hs = both[:, rows : rows + 2 * T].reshape(2, 2, T)
    hs = jnp.where(c == 0, hs, hs[::-1]).reshape(2 * NC, 1, T)
    own_scale = lax.dynamic_slice_in_dim(
        both[:, :rows].reshape(2, NX, per, 1, T), x, 1, axis=1
    )[:, 0]

    inc0 = incidence.reshape(NZ, NY, NC, T, T)
    inc1 = to_sibling(incidence).reshape(NZ, NY, NC, T, T)
    scaled = (row_scale[:, None] * features).astype(BF)
    scaled = scaled.reshape(blocks, T, NC, T).transpose(2, 0, 3, 1)
    st = jnp.concatenate(
        [
            lax.dynamic_index_in_dim(scaled, c, 0, keepdims=False),
            to_sibling(lax.dynamic_index_in_dim(scaled, 1 - c, 0, keepdims=False)),
        ]
    )
    pick = pick_first
    half = NZ // 2
    for applied in range(2):
        far = forward((2,), BF, z, y, code, pick, st, inc0, inc1)[0]
        up, down = along_y(far[:half], 1), along_y(far[half:], -1)
        near = forward((1, 3, 0), F32, z, y, code, pick, st, inc0, inc1)
        up, down = (
            along_y(low(near[0], up, half), 1),
            along_y(high(near[1], down, half), -1),
        )
        s = near[2] + up.astype(F32) + down.astype(F32)
        up, down = along_z(s[4, :NC].astype(BF), 1), along_z(s[4, NC:].astype(BF), -1)
        up, down = along_z(low(s[3], up, NC), 1), along_z(high(s[5], down, NC), -1)
        for k in (2, 1):
            up, down = (
                along_z((s[k] + up.astype(F32)).astype(BF), 1),
                along_z((s[NZ - k] + down.astype(F32)).astype(BF), -1),
            )
        hyper_sum = s[0] + up.astype(F32) + down.astype(F32)
        hyper = (hs * hyper_sum).astype(BF)

        found = [hyper] + [None] * (NZ - 1)
        up = down = hyper
        for k in range(1, half):
            up, down = along_z(up, 1), along_z(down, -1)
            found[NZ - k], found[k] = up, down
        found[half] = jnp.concatenate([along_z(up[:NC], 1), along_z(down[NC:], -1)])
        here = jnp.stack(found)
        up, down = along_y(here, 1), along_y(here, -1)
        all_z = ((0, NZ),)
        total = backward((0,), (all_z,), None, z, y, code, pick_rel, inc0, inc1, ((here,),))
        up2, down2 = along_y(up[:half], 1), along_y(down[half:], -1)
        total = backward(
            (1, 3), (all_z, all_z), total, z, y, code, pick_rel, inc0, inc1, ((down,), (up,))
        )
        total = backward(
            (2,),
            (((0, half), (half, half)),),
            total,
            z,
            y,
            code,
            pick_rel,
            inc0,
            inc1,
            ((up2, down2),),
        )

        part = total.reshape(NX, 2, per, T, T)
        up, down = along_x(part[2, :1].astype(BF), 1), along_x(part[2, 1:].astype(BF), -1)
        up, down = along_x(low(part[1], up, 1), 1), along_x(high(part[3], down, 1), -1)
        own_sum = part[0] + up.astype(F32) + down.astype(F32)
        current = own_scale * own_sum
        if applied == 0:
            own = (own_scale * current).astype(BF)
            up, down = along_x(own, 1), along_x(own, -1)
            across = jnp.concatenate([along_x(up[:1], 1), along_x(down[1:], -1)])
            st = jnp.stack([own, down, across, up]).reshape(2 * blocks, T, T)
            pick = pick_rel
    kept, came = current[0], to_sibling(current[1])
    pair = jnp.stack([jnp.where(c == 0, kept, came), jnp.where(c == 0, came, kept)])
    return pair.transpose(1, 3, 0, 2).reshape(per * T, NC * T)


def solution(mesh):
    placed = (
        P("vert", None),
        P("vert", None, "edge"),
        P("vert", "edge"),
        P("vert", "edge"),
        P("vert", "edge"),
        P("vert", "edge"),
        P("vert", "edge"),
        P("vert"),
    )
    return jax.shard_map(
        shards, mesh=mesh, in_specs=placed, out_specs=P(("vert", "edge"), None), check_vma=False
    )
```

```python
import functools

import jax
import jax.numpy as jnp
from jax import lax
from jax.experimental import pallas as pl
from jax.experimental.pallas import tpu as pltpu
from jax.sharding import PartitionSpec as P

NZ, NY, NC, NX = 8, 4, 2, 4
T = 128
SLOTS = NZ * NY * NC
BF = jnp.bfloat16
F32 = jnp.float32


def moved(dz, dy, flip):
    pairs = []
    for z in range(NZ):
        for y in range(NY):
            for c in range(NC):
                here = (z * NY + y) * NC + c
                there = (((z + dz) % NZ) * NY + (y + dy) % NY) * NC + (c ^ flip)
                pairs.append((here, there))
    return pairs


def along_z(a, step):
    return lax.ppermute(a, "vert", moved(step, 0, 0))


def along_y(a, step):
    return lax.ppermute(a, "vert", moved(0, step, 0))


def to_sibling(a):
    return lax.ppermute(a, "vert", moved(0, 0, 1))


def along_x(a, step):
    return lax.ppermute(a, "edge", [(i, (i + step) % NX) for i in range(NX)])


def turn_body(info, kept_in, sent_in, scale, kept, sent):
    kept[0] = (kept_in[...].T * scale[0]).astype(BF)
    sent[0] = (sent_in[...].T * scale[0]).astype(BF)


def turned(features, row_scale, c, x):
    blocks = features.shape[0] // T
    per = blocks // NX
    info = jnp.stack([c, 1 - c, x]).astype(jnp.int32)

    def place(i, info):
        return (lax.rem(i // per - info[2] + NX, NX) * per + lax.rem(i, per), 0, 0)

    return pl.pallas_call(
        turn_body,
        out_shape=[jax.ShapeDtypeStruct((blocks, T, T), BF)] * 2,
        grid_spec=pltpu.PrefetchScalarGridSpec(
            num_scalar_prefetch=1,
            grid=(blocks,),
            in_specs=[
                pl.BlockSpec((T, T), lambda i, info: (i, info[0])),
                pl.BlockSpec((T, T), lambda i, info: (i, info[1])),
                pl.BlockSpec((1, 1, T), lambda i, info: (i, 0, 0)),
            ],
            out_specs=[pl.BlockSpec((1, T, T), place)] * 2,
        ),
        name="turn_rows",
    )(info, features, features, row_scale.reshape(blocks, 1, T))


def forward_body(count, info, code, pick, st, *refs):
    z = info[0]
    for g in range(count):
        y_to = info[1 + g]
        inc0, inc1 = refs[2 * g], refs[2 * g + 1]
        for h in range(2):
            out = refs[2 * count + 2 * g + h]

            def one(i, carry, y_to=y_to, inc0=inc0, inc1=inc1, h=h, out=out):
                z_to = lax.rem(z + h * (NZ // 2) + i, NZ)
                for c in range(NC):
                    slot = (z_to * NY + y_to) * NC + c
                    a0 = st[pick[slot]]
                    a1 = st[pick[SLOTS + slot]]
                    k0 = code[slot]
                    k1 = code[SLOTS + slot]
                    zero = jnp.zeros_like(a0)
                    rows = [
                        jnp.concatenate(
                            [jnp.where(k0 == b, a0, zero), jnp.where(k1 == b, a1, zero)], axis=1
                        )
                        for b in range(2)
                    ]
                    left = jnp.concatenate(rows, axis=0)
                    right = jnp.concatenate([inc0[z_to, 0, c], inc1[z_to, 0, c]], axis=0)
                    got = jnp.dot(left, right, preferred_element_type=F32).astype(out.dtype)
                    out[i, 2 * c] = got[:T]
                    out[i, 2 * c + 1] = got[T:]
                return carry

            lax.fori_loop(0, NZ // 2, one, 0, unroll=2)


def forward(dys, dtype, z, y, code, pick, st, inc0, inc1):
    info = jnp.stack([z] + [(y + dy) % NY for dy in dys]).astype(jnp.int32)
    specs = [pl.BlockSpec((2 * 16, T, T), lambda i, *_: (0, 0, 0))]
    args = [st]
    for g in range(len(dys)):
        for inc in (inc0, inc1):
            specs.append(tile_spec(g))
            args.append(inc)
    half = (NZ // 2, 2 * NC, T, T)
    return pl.pallas_call(
        functools.partial(forward_body, len(dys)),
        out_shape=[jax.ShapeDtypeStruct(half, dtype)] * (2 * len(dys)),
        grid_spec=pltpu.PrefetchScalarGridSpec(
            num_scalar_prefetch=3,
            grid=(1,),
            in_specs=specs,
            out_specs=[pl.BlockSpec(half, lambda i, *_: (0, 0, 0, 0))] * (2 * len(dys)),
        ),
        name="tiles_forward",
    )(info, code, pick, *args)


def tile_spec(g):
    return pl.BlockSpec(
        (NZ, 1, NC, T, T), lambda i, info, code, pick: (0, info[1 + g], 0, 0, 0)
    )


def backward_body(count, first, last, info, code, pick, *refs):
    refs = list(refs)
    before = None if first else refs.pop(0)
    groups = [[refs.pop(0) for _ in range(4)] for _ in range(count)]
    total = refs.pop()
    if first:
        total[...] = jnp.zeros_like(total)
    else:
        total[...] = before[...]
    z = info[0]
    for g, (inc0, inc1, *halves) in enumerate(groups):
        y_to = info[1 + g]
        for h, held in enumerate(halves):

            def one(i, carry, y_to=y_to, inc=(inc0, inc1), h=h, held=held):
                z_to = lax.rem(z + h * (NZ // 2) + i, NZ)
                sums = []
                for c in range(NC):
                    slot = (z_to * NY + y_to) * NC + c
                    for s in range(2):
                        k = code[s * SLOTS + slot]
                        block = held[i, 2 * c + jnp.maximum(k, 0)]
                        block = jnp.where(k >= 0, block, jnp.zeros_like(block))
                        got = lax.dot_general(
                            block,
                            inc[s][z_to, 0, c],
                            (((1,), (1,)), ((), ())),
                            preferred_element_type=F32,
                        )
                        sums.append((pick[s * SLOTS + slot], got))
                for row, got in sums:
                    total[row] += got
                return carry

            lax.fori_loop(0, NZ // 2, one, 0)
    if last:
        own, *outs = refs
        own[...] = total[pl.ds(0, own.shape[0])]
        for n, out in enumerate(outs):
            size = out.shape[0]
            out[...] = total[pl.ds((n + 2) * size, size)].astype(BF)


def backward(dys, before, last, z, y, code, pick, inc0, inc1, helds):
    info = jnp.stack([z] + [(y + dy) % NY for dy in dys]).astype(jnp.int32)
    first = before is None
    blocks = 2 * 16
    per = blocks // (2 * NX)
    whole = pl.BlockSpec((blocks, T, T), lambda i, *_: (0, 0, 0))
    specs = [] if first else [whole]
    args = [] if first else [before]
    for g in range(len(dys)):
        for inc in (inc0, inc1):
            specs.append(tile_spec(g))
            args.append(inc)
        for held in helds[g]:
            specs.append(pl.BlockSpec(held.shape, lambda i, *_: (0, 0, 0, 0)))
            args.append(held)
    if last:
        shapes = [jax.ShapeDtypeStruct((2 * per, T, T), F32)]
        shapes += [jax.ShapeDtypeStruct((per, T, T), BF)] * (2 * (NX - 1))
        outs = [pl.BlockSpec(a.shape, lambda i, *_: (0, 0, 0)) for a in shapes]
        scratch = [pltpu.VMEM((blocks, T, T), F32)]
    else:
        shapes = jax.ShapeDtypeStruct((blocks, T, T), F32)
        outs = whole
        scratch = []
    return pl.pallas_call(
        functools.partial(backward_body, len(dys), first, last),
        out_shape=shapes,
        grid_spec=pltpu.PrefetchScalarGridSpec(
            num_scalar_prefetch=3,
            grid=(1,),
            in_specs=specs,
            out_specs=outs,
            scratch_shapes=scratch,
        ),
        name="tiles_backward",
    )(info, code, pick, *args)


def plus(a, b):
    return (a.astype(F32) + b.astype(F32)).astype(BF)


def low(a, b, m):
    return jnp.concatenate([a[:m] + b.astype(F32), a[m:]], axis=0).astype(BF)


def high(a, b, m):
    return jnp.concatenate([a[:m], a[m:] + b.astype(F32)], axis=0).astype(BF)


def shards(
    features, incidence, send_count, row_block, edge_block, edge_weight, edge_degree, vertex_degree
):
    vert = lax.axis_index("vert")
    x = lax.axis_index("edge")
    z, y, c = vert // (NY * NC), (vert // NC) % NY, vert % NC
    slots = SLOTS
    rows = features.shape[0]
    blocks = rows // T
    per = blocks // NX

    row_scale = 1.0 / jnp.sqrt(jnp.maximum(vertex_degree, 1).astype(F32))
    hyper_scale = edge_weight / jnp.maximum(edge_degree, 1).astype(F32)
    inc0 = incidence.reshape(NZ, NY, NC, T, T)
    inc1 = to_sibling(incidence).reshape(NZ, NY, NC, T, T)
    kept, sent = turned(features, row_scale, c, x)
    came = to_sibling(sent)
    mine = jnp.concatenate(
        [
            row_scale,
            hyper_scale.reshape(-1),
            send_count[:, 0].astype(F32),
            row_block[:, 0].astype(F32),
            edge_block[:, 0].astype(F32),
        ]
    )
    both = jnp.stack([mine, to_sibling(mine)])
    at = rows + 2 * T
    live = both[:, at : at + slots] > 0.5
    row_of = jnp.round(both[:, at + slots : at + 2 * slots]).astype(jnp.int32)
    edge_of = jnp.round(both[:, at + 2 * slots : at + 3 * slots]).astype(jnp.int32)
    code = jnp.where(live, edge_of, -1).reshape(-1)
    side = jnp.arange(2, dtype=jnp.int32)[:, None]
    pick = ((((row_of // per) - x) % NX) * 2 * per + side * per + row_of % per).reshape(-1)
    hs = both[:, rows : rows + 2 * T].reshape(2, 2, T)
    hs = jnp.where(c == 0, hs, hs[::-1]).reshape(2 * NC, 1, T)
    own_scale = lax.dynamic_slice_in_dim(
        both[:, :rows].reshape(2, NX, per, 1, T), x, 1, axis=1
    ).reshape(2 * per, 1, T)
    st = jnp.stack(
        [kept.reshape(NX, per, T, T), came.reshape(NX, per, T, T)], axis=1
    ).reshape(2 * blocks, T, T)

    at_tiles = (z, y, code, pick)
    half = NZ // 2

    def apply(applied, carry):
        st, _ = carry
        a2, b2 = forward((2,), BF, *at_tiles, st, inc0, inc1)
        a2, b2 = along_y(a2, 1), along_y(b2, -1)
        a1, b1, a3, b3 = forward((1, 3), BF, *at_tiles, st, inc0, inc1)
        up_b, down_a = along_y(b1, 1), along_y(a3, -1)
        a0, b0 = forward((0,), F32, *at_tiles, st, inc0, inc1)
        up_a, down_b = along_y(plus(a1, a2), 1), along_y(plus(b3, b2), -1)
        a = a0 + up_a.astype(F32) + down_a.astype(F32)
        b = b0 + up_b.astype(F32) + down_b.astype(F32)
        s = [a[k] for k in range(half)] + [b[k] for k in range(half)]
        up, down = along_z(s[4][:NC].astype(BF), 1), along_z(s[4][NC:].astype(BF), -1)
        up, down = along_z(low(s[3], up, NC), 1), along_z(high(s[5], down, NC), -1)
        for k in (2, 1):
            up, down = along_z(plus(s[k], up), 1), along_z(plus(s[NZ - k], down), -1)
        hyper_sum = s[0] + up.astype(F32) + down.astype(F32)
        hyper = (hs * hyper_sum).astype(BF)

        found = [hyper] + [None] * (NZ - 1)
        up = down = hyper
        for k in range(1, half):
            up, down = along_z(up, 1), along_z(down, -1)
            found[NZ - k], found[k] = up, down
        here_a = jnp.stack(found[:half])
        found[half] = jnp.concatenate([along_z(up[:NC], 1), along_z(down[NC:], -1)])
        up_a, down_a = along_y(here_a, 1), along_y(here_a, -1)
        here_b = jnp.stack(found[half:])
        up_b, down_b = along_y(here_b, 1), along_y(here_b, -1)
        total = backward((0,), None, False, *at_tiles, inc0, inc1, ((here_a, here_b),))
        up_a, down_b, total = lax.optimization_barrier((up_a, down_b, total))
        far_a, far_b = along_y(up_a, 1), along_y(down_b, -1)
        total = backward(
            (3, 1), total, False, *at_tiles, inc0, inc1, ((up_a, up_b), (down_a, down_b))
        )
        own, p1, q1, p2, q2, p3, q3 = backward(
            (2,), total, True, *at_tiles, inc0, inc1, ((far_a, far_b),)
        )

        p2, q2 = along_x(p2, 1), along_x(q2, -1)
        up_q, down_p = along_x(q1, 1), along_x(p3, -1)
        up_p, down_q = along_x(plus(p1, p2), 1), along_x(plus(q3, q2), -1)
        up = jnp.concatenate([up_p, up_q]).astype(F32)
        down = jnp.concatenate([down_p, down_q]).astype(F32)
        current = own_scale * (own + up + down)

        def spread(current):
            own = (own_scale * current).astype(BF)
            up, down = along_x(own, 1), along_x(own, -1)
            across = [along_x(up[:per], 1), along_x(down[per:], -1)]
            return jnp.concatenate([own, down, *across, up])

        st = lax.cond(applied == 0, spread, lambda _: st, current)
        return st, current

    _, current = lax.fori_loop(0, 2, apply, (st, jnp.zeros((2 * per, T, T), F32)))
    kept, came = current[:per], to_sibling(current[per:])
    pair = jnp.stack([jnp.where(c == 0, kept, came), jnp.where(c == 0, came, kept)])
    return pair.transpose(1, 3, 0, 2).reshape(per * T, NC * T)


def solution(mesh):
    placed = (
        P("vert", None),
        P("vert", None, "edge"),
        P("vert", "edge"),
        P("vert", "edge"),
        P("vert", "edge"),
        P("vert", "edge"),
        P("vert", "edge"),
        P("vert"),
    )
    return jax.shard_map(
        shards, mesh=mesh, in_specs=placed, out_specs=P(("vert", "edge"), None), check_vma=False
    )
```

```python
import functools

import jax
import jax.numpy as jnp
from jax import lax
from jax.experimental import pallas as pl
from jax.experimental.pallas import tpu as pltpu
from jax.sharding import PartitionSpec as P

NZ, NY, NC, NX = 8, 4, 2, 4
T = 128
SLOTS = NZ * NY * NC
BF = jnp.bfloat16
F32 = jnp.float32


def moved(dz, dy, flip):
    pairs = []
    for z in range(NZ):
        for y in range(NY):
            for c in range(NC):
                here = (z * NY + y) * NC + c
                there = (((z + dz) % NZ) * NY + (y + dy) % NY) * NC + (c ^ flip)
                pairs.append((here, there))
    return pairs


def along_z(a, step):
    return lax.ppermute(a, "vert", moved(step, 0, 0))


def along_y(a, step):
    return lax.ppermute(a, "vert", moved(0, step, 0))


def to_sibling(a):
    return lax.ppermute(a, "vert", moved(0, 0, 1))


def along_x(a, step):
    return lax.ppermute(a, "edge", [(i, (i + step) % NX) for i in range(NX)])


def turn_body(info, kept_in, sent_in, scale, kept, sent):
    for r in range(scale.shape[0]):
        rows = pl.ds(r * T, T)
        kept[r] = (kept_in[rows].T * scale[r]).astype(BF)
        sent[r] = (sent_in[rows].T * scale[r]).astype(BF)


def turned(features, row_scale, c):
    blocks = features.shape[0] // T
    per = 4
    info = jnp.stack([c, 1 - c]).astype(jnp.int32)
    return pl.pallas_call(
        turn_body,
        out_shape=[jax.ShapeDtypeStruct((blocks, T, T), BF)] * 2,
        grid_spec=pltpu.PrefetchScalarGridSpec(
            num_scalar_prefetch=1,
            grid=(blocks // per,),
            in_specs=[
                pl.BlockSpec((per * T, T), lambda i, info: (i, info[0])),
                pl.BlockSpec((per * T, T), lambda i, info: (i, info[1])),
                pl.BlockSpec((per, 1, T), lambda i, info: (i, 0, 0)),
            ],
            out_specs=[pl.BlockSpec((per, T, T), lambda i, info: (i, 0, 0))] * 2,
        ),
        name="turn_rows",
    )(info, features, features, row_scale.reshape(blocks, 1, T))


def forward_body(count, info, code, pick, st, *refs):
    z = info[0]
    for g in range(count):
        y_to = info[1 + g]
        inc0, inc1 = refs[2 * g], refs[2 * g + 1]
        for h in range(2):
            out = refs[2 * count + 2 * g + h]

            def one(i, carry, y_to=y_to, inc0=inc0, inc1=inc1, h=h, out=out):
                z_to = lax.rem(z + h * (NZ // 2) + i, NZ)
                for c in range(NC):
                    slot = (z_to * NY + y_to) * NC + c
                    a0 = st[pick[slot]]
                    a1 = st[pick[SLOTS + slot]]
                    k0 = code[slot]
                    k1 = code[SLOTS + slot]
                    t0 = inc0[z_to, 0, c]
                    t1 = inc1[z_to, 0, c]
                    zero = jnp.zeros_like(t0)
                    left = jnp.concatenate([a0, a1], axis=1)
                    columns = [
                        jnp.concatenate(
                            [jnp.where(k0 == b, t0, zero), jnp.where(k1 == b, t1, zero)], axis=0
                        )
                        for b in range(2)
                    ]
                    right = jnp.concatenate(columns, axis=1)
                    got = jnp.dot(left, right, preferred_element_type=F32).astype(out.dtype)
                    out[i, 2 * c] = got[:, :T]
                    out[i, 2 * c + 1] = got[:, T:]
                return carry

            lax.fori_loop(0, NZ // 2, one, 0, unroll=4)


def forward(dys, dtype, z, y, code, pick, st, inc0, inc1):
    info = jnp.stack([z] + [(y + dy) % NY for dy in dys]).astype(jnp.int32)
    specs = [pl.BlockSpec((2 * 16, T, T), lambda i, *_: (0, 0, 0))]
    args = [st]
    for g in range(len(dys)):
        for inc in (inc0, inc1):
            specs.append(tile_spec(g))
            args.append(inc)
    half = (NZ // 2, 2 * NC, T, T)
    return pl.pallas_call(
        functools.partial(forward_body, len(dys)),
        out_shape=[jax.ShapeDtypeStruct(half, dtype)] * (2 * len(dys)),
        grid_spec=pltpu.PrefetchScalarGridSpec(
            num_scalar_prefetch=3,
            grid=(1,),
            in_specs=specs,
            out_specs=[pl.BlockSpec(half, lambda i, *_: (0, 0, 0, 0))] * (2 * len(dys)),
        ),
        name="tiles_forward",
    )(info, code, pick, *args)


def tile_spec(g):
    return pl.BlockSpec(
        (NZ, 1, NC, T, T), lambda i, info, code, pick: (0, info[1 + g], 0, 0, 0)
    )


def backward_body(count, first, info, code, pick, *refs):
    refs = list(refs)
    before = None if first else refs.pop(0)
    groups = [[refs.pop(0) for _ in range(4)] for _ in range(count)]
    total = refs.pop()
    if first:
        total[...] = jnp.zeros_like(total)
    else:
        total[...] = before[...]
    z = info[0]
    for g, (inc0, inc1, *halves) in enumerate(groups):
        y_to = info[1 + g]
        for h, held in enumerate(halves):

            def one(i, carry, y_to=y_to, inc=(inc0, inc1), h=h, held=held):
                z_to = lax.rem(z + h * (NZ // 2) + i, NZ)
                sums = []
                for c in range(NC):
                    slot = (z_to * NY + y_to) * NC + c
                    for s in range(2):
                        k = code[s * SLOTS + slot]
                        block = held[i, 2 * c + jnp.maximum(k, 0)]
                        block = jnp.where(k >= 0, block, jnp.zeros_like(block))
                        got = lax.dot_general(
                            block,
                            inc[s][z_to, 0, c],
                            (((1,), (1,)), ((), ())),
                            preferred_element_type=F32,
                        )
                        sums.append((pick[s * SLOTS + slot], got))
                for row, got in sums:
                    total[row] += got
                return carry

            lax.fori_loop(0, NZ // 2, one, 0, unroll=4)
    start = 0
    for out in refs:
        size = out.shape[0]
        out[...] = total[pl.ds(start, size)].astype(out.dtype)
        start += size


def backward(dys, before, outs, z, y, code, pick, inc0, inc1, helds):
    info = jnp.stack([z] + [(y + dy) % NY for dy in dys]).astype(jnp.int32)
    first = before is None
    blocks = 2 * 16
    whole = pl.BlockSpec((blocks, T, T), lambda i, *_: (0, 0, 0))
    specs = [] if first else [whole]
    args = [] if first else [before]
    for g in range(len(dys)):
        for inc in (inc0, inc1):
            specs.append(tile_spec(g))
            args.append(inc)
        for held in helds[g]:
            specs.append(pl.BlockSpec(held.shape, lambda i, *_: (0, 0, 0, 0)))
            args.append(held)
    if outs:
        shapes = [jax.ShapeDtypeStruct((n, T, T), dtype) for n, dtype in outs]
        out_specs = [pl.BlockSpec(a.shape, lambda i, *_: (0, 0, 0)) for a in shapes]
        scratch = [pltpu.VMEM((blocks, T, T), F32)]
    else:
        shapes = jax.ShapeDtypeStruct((blocks, T, T), F32)
        out_specs = whole
        scratch = []
    return pl.pallas_call(
        functools.partial(backward_body, len(dys), first),
        out_shape=shapes,
        grid_spec=pltpu.PrefetchScalarGridSpec(
            num_scalar_prefetch=3,
            grid=(1,),
            in_specs=specs,
            out_specs=out_specs,
            scratch_shapes=scratch,
        ),
        name="tiles_backward",
    )(info, code, pick, *args)


def plus(a, b):
    return (a.astype(F32) + b.astype(F32)).astype(BF)


def shards(
    features, incidence, send_count, row_block, edge_block, edge_weight, edge_degree, vertex_degree
):
    vert = lax.axis_index("vert")
    x = lax.axis_index("edge")
    z, y, c = vert // (NY * NC), (vert // NC) % NY, vert % NC
    slots = SLOTS
    rows = features.shape[0]
    blocks = rows // T
    per = blocks // NX

    row_scale = 1.0 / jnp.sqrt(jnp.maximum(vertex_degree, 1).astype(F32))
    hyper_scale = edge_weight / jnp.maximum(edge_degree, 1).astype(F32)
    inc0 = incidence.reshape(NZ, NY, NC, T, T)
    inc1 = to_sibling(incidence).reshape(NZ, NY, NC, T, T)
    kept, sent = turned(features, row_scale, c)
    st = jnp.concatenate([kept, to_sibling(sent)])
    mine = jnp.concatenate(
        [
            row_scale,
            hyper_scale.reshape(-1),
            send_count[:, 0].astype(F32),
            row_block[:, 0].astype(F32),
            edge_block[:, 0].astype(F32),
        ]
    )
    both = jnp.stack([mine, to_sibling(mine)])
    at = rows + 2 * T
    live = both[:, at : at + slots] > 0.5
    row_of = jnp.round(both[:, at + slots : at + 2 * slots]).astype(jnp.int32)
    edge_of = jnp.round(both[:, at + 2 * slots : at + 3 * slots]).astype(jnp.int32)
    code = jnp.where(live, edge_of, -1).reshape(-1)
    side = jnp.arange(2, dtype=jnp.int32)[:, None]
    pick = (side * blocks + row_of).reshape(-1)
    pick_share = ((((row_of // per) - x) % NX) * 2 * per + side * per + row_of % per).reshape(-1)
    hs = both[:, rows : rows + 2 * T].reshape(2, 2, T)
    hs = jnp.where(c == 0, hs, hs[::-1]).reshape(2 * NC, 1, T)
    scale = both[:, :rows].reshape(2 * blocks, 1, T)
    own_scale = lax.dynamic_slice_in_dim(
        both[:, :rows].reshape(2, NX, per, 1, T), x, 1, axis=1
    ).reshape(2 * per, 1, T)

    half = NZ // 2
    for applied in range(2):
        at_tiles = (z, y, code, pick)
        a2, b2 = forward((2,), BF, *at_tiles, st, inc0, inc1)
        a2, b2 = along_y(a2, 1), along_y(b2, -1)
        a1, b1, a3, b3 = forward((1, 3), BF, *at_tiles, st, inc0, inc1)
        up_b, down_a = along_y(b1, 1), along_y(a3, -1)
        a0, b0 = forward((0,), F32, *at_tiles, st, inc0, inc1)
        up_a, down_b = along_y(plus(a1, a2), 1), along_y(plus(b3, b2), -1)
        a = a0 + up_a.astype(F32) + down_a.astype(F32)
        b = b0 + up_b.astype(F32) + down_b.astype(F32)
        near_up = jnp.stack([a[3], a[1]]).astype(BF)
        near_down = jnp.stack([b[1], b[3]]).astype(BF)
        near_up, near_down = along_z(near_up, 1), along_z(near_down, -1)
        far_up, far_down = along_z(b[0, :NC].astype(BF), 2), along_z(b[0, NC:].astype(BF), -2)
        near_up, near_down = near_up.astype(F32), near_down.astype(F32)
        far_up = jnp.pad(far_up.astype(F32), ((0, NC), (0, 0), (0, 0)))
        far_down = jnp.pad(far_down.astype(F32), ((NC, 0), (0, 0), (0, 0)))
        up = along_z((a[2] + near_up[0] + far_up).astype(BF), 2)
        down = along_z((b[2] + near_down[0] + far_down).astype(BF), -2)
        hyper_sum = a[0] + near_up[1] + near_down[1] + up.astype(F32) + down.astype(F32)
        hyper = (hs * hyper_sum).astype(BF)

        up2, down2 = along_z(hyper, 2), along_z(hyper, -2)
        up = along_z(jnp.stack([hyper, up2]), 1)
        down = along_z(jnp.stack([hyper, down2]), -1)
        across = jnp.concatenate([along_z(up2[:NC], 2), along_z(down2[NC:], -2)])
        here_a = jnp.stack([hyper, down[0], down2, down[1]])
        up_a, down_a = along_y(here_a, 1), along_y(here_a, -1)
        here_b = jnp.stack([across, up[1], up2, up[0]])
        up_b, down_b = along_y(here_b, 1), along_y(here_b, -1)
        if applied == 1:
            at_tiles = (z, y, code, pick_share)
        total = backward((0,), None, None, *at_tiles, inc0, inc1, ((here_a, here_b),))
        up_a, down_b, total = lax.optimization_barrier((up_a, down_b, total))
        far_a, far_b = along_y(up_a, 1), along_y(down_b, -1)
        total = backward(
            (3, 1), total, None, *at_tiles, inc0, inc1, ((up_a, up_b), (down_a, down_b))
        )
        if applied == 0:
            outs = [(blocks, BF)] * 2
        else:
            outs = [(2 * per, F32)] + [(per, BF)] * (2 * (NX - 1))
        parts = backward((2,), total, outs, *at_tiles, inc0, inc1, ((far_a, far_b),))
        if applied == 0:
            p, q = parts
            up_p, down_q = along_x(p, 1), along_x(q, -1)
            up_q, down_p = along_x(q, 1), along_x(p, -1)
            far_p, far_q = along_x(up_p, 1), along_x(down_q, -1)
            sums = [
                sum(n.astype(F32) for n in group)
                for group in ((p, up_p, down_p, far_p), (q, up_q, down_q, far_q))
            ]
            st = (scale * (scale * jnp.concatenate(sums))).astype(BF)
    own, p1, q1, p2, q2, p3, q3 = parts
    p2, q2 = along_x(p2, 1), along_x(q2, -1)
    up_q, down_p = along_x(q1, 1), along_x(p3, -1)
    up_p, down_q = along_x(plus(p1, p2), 1), along_x(plus(q3, q2), -1)
    up = jnp.concatenate([up_p, up_q]).astype(F32)
    down = jnp.concatenate([down_p, down_q]).astype(F32)
    current = own_scale * (own + up + down)
    kept, came = current[:per], to_sibling(current[per:])
    pair = jnp.stack([jnp.where(c == 0, kept, came), jnp.where(c == 0, came, kept)])
    return pair.transpose(1, 3, 0, 2).reshape(per * T, NC * T)


def solution(mesh):
    placed = (
        P("vert", None),
        P("vert", None, "edge"),
        P("vert", "edge"),
        P("vert", "edge"),
        P("vert", "edge"),
        P("vert", "edge"),
        P("vert", "edge"),
        P("vert"),
    )
    return jax.shard_map(
        shards, mesh=mesh, in_specs=placed, out_specs=P(("vert", "edge"), None), check_vma=False
    )
```

```python
import functools

import jax
import jax.numpy as jnp
from jax import lax
from jax.experimental import pallas as pl
from jax.experimental.pallas import tpu as pltpu
from jax.sharding import PartitionSpec as P


NZ, NY, NC, NX = 8, 4, 2, 4
T = 128
SLOTS = NZ * NY * NC
VMEM = 16 << 20
WHOLE = pl.BlockSpec(memory_space=pltpu.VMEM)
BF = jnp.bfloat16
F32 = jnp.float32


def moved(dz, dy, flip):
    pairs = []
    for z in range(NZ):
        for y in range(NY):
            for c in range(NC):
                here = (z * NY + y) * NC + c
                there = (((z + dz) % NZ) * NY + (y + dy) % NY) * NC + (c ^ flip)
                pairs.append((here, there))
    return pairs


def along_z(a, step):
    return lax.ppermute(a, "vert", moved(step, 0, 0))


def along_y(a, step):
    return lax.ppermute(a, "vert", moved(0, step, 0))


def to_sibling(a):
    return lax.ppermute(a, "vert", moved(0, 0, 1))


def along_x(a, step):
    return lax.ppermute(a, "edge", [(i, (i + step) % NX) for i in range(NX)])


def turn_body(info, kept_in, sent_in, scale, kept, sent):
    for r in range(scale.shape[0]):
        rows = pl.ds(r * T, T)
        kept[r] = (kept_in[rows].T * scale[r]).astype(BF)
        sent[r] = (sent_in[rows].T * scale[r]).astype(BF)


def turned(features, row_scale, c):
    blocks = features.shape[0] // T
    per = 4
    info = jnp.stack([c, 1 - c]).astype(jnp.int32)
    return pl.pallas_call(
        turn_body,
        out_shape=[jax.ShapeDtypeStruct((blocks, T, T), BF)] * 2,
        grid_spec=pltpu.PrefetchScalarGridSpec(
            num_scalar_prefetch=1,
            grid=(blocks // per,),
            in_specs=[
                pl.BlockSpec((per * T, T), lambda i, info: (i, info[0])),
                pl.BlockSpec((per * T, T), lambda i, info: (i, info[1])),
                pl.BlockSpec((per, 1, T), lambda i, info: (i, 0, 0)),
            ],
            out_specs=[pl.BlockSpec((per, T, T), lambda i, info: (i, 0, 0))] * 2,
        ),
        compiler_params=pltpu.CompilerParams(vmem_limit_bytes=8 << 20),
        name="turn_rows",
    )(info, features, features, row_scale.reshape(blocks, 1, T))


def forward_body(count, info, code, pick, st0, st1, *refs):
    z = info[0]
    for g in range(count):
        y_to = info[1 + g]
        inc0, inc1 = refs[2 * g], refs[2 * g + 1]
        for h in range(2):
            out = refs[2 * count + 2 * g + h]

            def one(i, carry, y_to=y_to, inc0=inc0, inc1=inc1, h=h, out=out):
                z_to = lax.rem(z + h * (NZ // 2) + i, NZ)
                for c in range(NC):
                    slot = (z_to * NY + y_to) * NC + c
                    a0 = st0[pick[slot]]
                    a1 = st1[pick[SLOTS + slot]]
                    k0 = code[slot]
                    k1 = code[SLOTS + slot]
                    t0 = inc0[z_to, 0, c]
                    t1 = inc1[z_to, 0, c]
                    zero = jnp.zeros_like(t0)
                    left = jnp.concatenate([a0, a1], axis=1)
                    columns = [
                        jnp.concatenate(
                            [jnp.where(k0 == b, t0, zero), jnp.where(k1 == b, t1, zero)], axis=0
                        )
                        for b in range(2)
                    ]
                    right = jnp.concatenate(columns, axis=1)
                    got = jnp.dot(left, right, preferred_element_type=F32).astype(out.dtype)
                    out[i, 2 * c] = got[:, :T]
                    out[i, 2 * c + 1] = got[:, T:]
                return carry

            lax.fori_loop(0, NZ // 2, one, 0, unroll=4)


def forward(dys, dtype, z, y, code, pick, st, inc0, inc1):
    info = jnp.stack([z] + [(y + dy) % NY for dy in dys]).astype(jnp.int32)
    specs = [WHOLE] * len(st)
    args = [*st]
    for g in range(len(dys)):
        for inc in (inc0, inc1):
            specs.append(tile_spec(g))
            args.append(inc)
    half = (NZ // 2, 2 * NC, T, T)
    return pl.pallas_call(
        functools.partial(forward_body, len(dys)),
        out_shape=[jax.ShapeDtypeStruct(half, dtype)] * (2 * len(dys)),
        grid_spec=pltpu.PrefetchScalarGridSpec(
            num_scalar_prefetch=3,
            grid=(1,),
            in_specs=specs,
            out_specs=[WHOLE] * (2 * len(dys)),
        ),
        compiler_params=pltpu.CompilerParams(vmem_limit_bytes=VMEM),
        name="tiles_forward",
    )(info, code, pick, *args)


def tile_spec(g):
    return pl.BlockSpec(
        (NZ, 1, NC, T, T), lambda i, info, code, pick: (0, info[1 + g], 0, 0, 0)
    )


def backward_body(count, first, info, code, pick, *refs):
    refs = list(refs)
    before = None if first else refs.pop(0)
    groups = [[refs.pop(0) for _ in range(4)] for _ in range(count)]
    total = refs.pop()
    if first:
        total[...] = jnp.zeros_like(total)
    else:
        total[...] = before[...]
    z = info[0]
    for g, (inc0, inc1, *halves) in enumerate(groups):
        y_to = info[1 + g]
        for h, held in enumerate(halves):

            def one(i, carry, y_to=y_to, inc=(inc0, inc1), h=h, held=held):
                z_to = lax.rem(z + h * (NZ // 2) + i, NZ)
                sums = []
                for c in range(NC):
                    slot = (z_to * NY + y_to) * NC + c
                    for s in range(2):
                        k = code[s * SLOTS + slot]
                        block = held[i, 2 * c + jnp.maximum(k, 0)]
                        block = jnp.where(k >= 0, block, jnp.zeros_like(block))
                        got = lax.dot_general(
                            block,
                            inc[s][z_to, 0, c],
                            (((1,), (1,)), ((), ())),
                            preferred_element_type=F32,
                        )
                        sums.append((pick[s * SLOTS + slot], got))
                for row, got in sums:
                    total[row] += got
                return carry

            lax.fori_loop(0, NZ // 2, one, 0, unroll=4)
    start = 0
    for out in refs:
        size = out.shape[0]
        out[...] = total[pl.ds(start, size)].astype(out.dtype)
        start += size


def backward(dys, before, outs, z, y, code, pick, inc0, inc1, helds):
    info = jnp.stack([z] + [(y + dy) % NY for dy in dys]).astype(jnp.int32)
    first = before is None
    blocks = 2 * 16
    specs = [] if first else [WHOLE]
    args = [] if first else [before]
    for g in range(len(dys)):
        for inc in (inc0, inc1):
            specs.append(tile_spec(g))
            args.append(inc)
        for held in helds[g]:
            specs.append(WHOLE)
            args.append(held)
    if outs:
        shapes = [jax.ShapeDtypeStruct((n, T, T), dtype) for n, dtype in outs]
        out_specs = [WHOLE] * len(shapes)
        scratch = [pltpu.VMEM((blocks, T, T), F32)]
    else:
        shapes = jax.ShapeDtypeStruct((blocks, T, T), F32)
        out_specs = WHOLE
        scratch = []
    return pl.pallas_call(
        functools.partial(backward_body, len(dys), first),
        out_shape=shapes,
        grid_spec=pltpu.PrefetchScalarGridSpec(
            num_scalar_prefetch=3,
            grid=(1,),
            in_specs=specs,
            out_specs=out_specs,
            scratch_shapes=scratch,
        ),
        compiler_params=pltpu.CompilerParams(vmem_limit_bytes=VMEM),
        name="tiles_backward",
    )(info, code, pick, *args)


def plus(a, b):
    return (a.astype(F32) + b.astype(F32)).astype(BF)


def shards(
    features, incidence, send_count, row_block, edge_block, edge_weight, edge_degree, vertex_degree
):
    vert = lax.axis_index("vert")
    x = lax.axis_index("edge")
    z, y, c = vert // (NY * NC), (vert // NC) % NY, vert % NC
    slots = SLOTS
    rows = features.shape[0]
    blocks = rows // T
    per = blocks // NX

    row_scale = 1.0 / jnp.sqrt(jnp.maximum(vertex_degree, 1).astype(F32))
    hyper_scale = edge_weight / jnp.maximum(edge_degree, 1).astype(F32)
    inc0 = incidence.reshape(NZ, NY, NC, T, T)
    inc1 = to_sibling(incidence).reshape(NZ, NY, NC, T, T)
    kept, sent = turned(features, row_scale, c)
    st = (kept, to_sibling(sent))
    mine = jnp.concatenate(
        [
            row_scale,
            hyper_scale.reshape(-1),
            send_count[:, 0].astype(F32),
            row_block[:, 0].astype(F32),
            edge_block[:, 0].astype(F32),
        ]
    )
    both = jnp.stack([mine, to_sibling(mine)])
    at = rows + 2 * T
    live = both[:, at : at + slots] > 0.5
    row_of = jnp.round(both[:, at + slots : at + 2 * slots]).astype(jnp.int32)
    edge_of = jnp.round(both[:, at + 2 * slots : at + 3 * slots]).astype(jnp.int32)
    code = jnp.where(live, edge_of, -1).reshape(-1)
    side = jnp.arange(2, dtype=jnp.int32)[:, None]
    row_of_flat = row_of.reshape(-1)
    pick = (side * blocks + row_of).reshape(-1)
    pick_share = ((((row_of // per) - x) % NX) * 2 * per + side * per + row_of % per).reshape(-1)
    hs = both[:, rows : rows + 2 * T].reshape(2, 2, T)
    hs = jnp.where(c == 0, hs, hs[::-1]).reshape(2 * NC, 1, T)
    scale = both[:, :rows].reshape(2, blocks, 1, T)
    own_scale = lax.dynamic_slice_in_dim(
        both[:, :rows].reshape(2, NX, per, 1, T), x, 1, axis=1
    ).reshape(2 * per, 1, T)

    for applied in range(2):
        at_tiles = (z, y, code, row_of_flat)
        a2, b2 = forward((2,), BF, *at_tiles, st, inc0, inc1)
        a2, b2 = along_y(a2, 1), along_y(b2, -1)
        a1, b1, a3, b3 = forward((1, 3), BF, *at_tiles, st, inc0, inc1)
        up_b, down_a = along_y(b1, 1), along_y(a3, -1)
        a0, b0 = forward((0,), F32, *at_tiles, st, inc0, inc1)
        up_a, down_b = along_y(plus(a1, a2), 1), along_y(plus(b3, b2), -1)
        a = a0 + up_a.astype(F32) + down_a.astype(F32)
        b = b0 + up_b.astype(F32) + down_b.astype(F32)
        near_up = jnp.stack([a[3], a[1]]).astype(BF)
        near_down = jnp.stack([b[1], b[3]]).astype(BF)
        near_up, near_down = along_z(near_up, 1), along_z(near_down, -1)
        far_up, far_down = along_z(b[0, :NC].astype(BF), 2), along_z(b[0, NC:].astype(BF), -2)
        near_up, near_down = near_up.astype(F32), near_down.astype(F32)
        far_up = jnp.pad(far_up.astype(F32), ((0, NC), (0, 0), (0, 0)))
        far_down = jnp.pad(far_down.astype(F32), ((NC, 0), (0, 0), (0, 0)))
        up = along_z((a[2] + near_up[0] + far_up).astype(BF), 2)
        down = along_z((b[2] + near_down[0] + far_down).astype(BF), -2)
        hyper_sum = a[0] + near_up[1] + near_down[1] + up.astype(F32) + down.astype(F32)
        hyper = (hs * hyper_sum).astype(BF)

        up2, down2 = along_z(hyper, 2), along_z(hyper, -2)
        up = along_z(jnp.stack([hyper, up2]), 1)
        down = along_z(jnp.stack([hyper, down2]), -1)
        across = jnp.concatenate([along_z(up2[:NC], 2), along_z(down2[NC:], -2)])
        here_a = jnp.stack([hyper, down[0], down2, down[1]])
        up_a, down_a = along_y(here_a, 1), along_y(here_a, -1)
        here_b = jnp.stack([across, up[1], up2, up[0]])
        up_b, down_b = along_y(here_b, 1), along_y(here_b, -1)
        at_tiles = (z, y, code, pick if applied == 0 else pick_share)
        total = backward((0,), None, None, *at_tiles, inc0, inc1, ((here_a, here_b),))
        up_a, down_b, total = lax.optimization_barrier((up_a, down_b, total))
        far_a, far_b = along_y(up_a, 1), along_y(down_b, -1)
        total = backward(
            (3, 1), total, None, *at_tiles, inc0, inc1, ((up_a, up_b), (down_a, down_b))
        )
        if applied == 0:
            outs = [(blocks, BF)] * 2
        else:
            outs = [(2 * per, F32)] + [(per, BF)] * (2 * (NX - 1))
        parts = backward((2,), total, outs, *at_tiles, inc0, inc1, ((far_a, far_b),))
        if applied == 0:
            p, q = parts
            up_p, down_q = along_x(p, 1), along_x(q, -1)
            up_q, down_p = along_x(q, 1), along_x(p, -1)
            far_p, far_q = along_x(up_p, 1), along_x(down_q, -1)
            st = tuple(
                (r * (r * sum(n.astype(F32) for n in group))).astype(BF)
                for r, group in zip(scale, ((p, up_p, down_p, far_p), (q, up_q, down_q, far_q)))
            )
    own, p1, q1, p2, q2, p3, q3 = parts
    p2, q2 = along_x(p2, 1), along_x(q2, -1)
    up_q, down_p = along_x(q1, 1), along_x(p3, -1)
    up_p, down_q = along_x(plus(p1, p2), 1), along_x(plus(q3, q2), -1)
    up = jnp.concatenate([up_p, up_q]).astype(F32)
    down = jnp.concatenate([down_p, down_q]).astype(F32)
    current = own_scale * (own + up + down)
    kept, came = current[:per], to_sibling(current[per:])
    pair = jnp.stack([jnp.where(c == 0, kept, came), jnp.where(c == 0, came, kept)])
    return pair.transpose(1, 3, 0, 2).reshape(per * T, NC * T)


def solution(mesh):
    placed = (
        P("vert", None),
        P("vert", None, "edge"),
        P("vert", "edge"),
        P("vert", "edge"),
        P("vert", "edge"),
        P("vert", "edge"),
        P("vert", "edge"),
        P("vert"),
    )
    return jax.shard_map(
        shards, mesh=mesh, in_specs=placed, out_specs=P(("vert", "edge"), None), check_vma=False
    )
```

```python
import functools

import jax
import jax.numpy as jnp
from jax import lax
from jax.experimental import pallas as pl
from jax.experimental.pallas import tpu as pltpu
from jax.sharding import PartitionSpec as P


NZ, NY, NC, NX = 8, 4, 2, 4
T = 128
SLOTS = NZ * NY * NC
VMEM = 16 << 20
WHOLE = pl.BlockSpec(memory_space=pltpu.VMEM)
BF = jnp.bfloat16
F32 = jnp.float32


def moved(dz, dy, flip):
    pairs = []
    for z in range(NZ):
        for y in range(NY):
            for c in range(NC):
                here = (z * NY + y) * NC + c
                there = (((z + dz) % NZ) * NY + (y + dy) % NY) * NC + (c ^ flip)
                pairs.append((here, there))
    return pairs


def along_z(a, step):
    return lax.ppermute(a, "vert", moved(step, 0, 0))


def along_y(a, step):
    return lax.ppermute(a, "vert", moved(0, step, 0))


def to_sibling(a):
    return lax.ppermute(a, "vert", moved(0, 0, 1))


def along_x(a, step):
    return lax.ppermute(a, "edge", [(i, (i + step) % NX) for i in range(NX)])


def turn_body(per, here, kept_in, sent_in, scale, kept, sent):
    for r in range(per):
        rows = pl.ds(r * T, T)
        by = scale[pl.ds(pl.program_id(0) * per + r, 1)]
        kept[r] = (kept_in[rows].T * by).astype(BF)
        sent[r] = (sent_in[rows].T * by).astype(BF)


def turned(features, row_scale, here):
    blocks = features.shape[0] // T
    per = 4
    return pl.pallas_call(
        functools.partial(turn_body, per),
        out_shape=[jax.ShapeDtypeStruct((blocks, T, T), BF)] * 2,
        grid_spec=pltpu.PrefetchScalarGridSpec(
            num_scalar_prefetch=1,
            grid=(blocks // per,),
            in_specs=[
                pl.BlockSpec((per * T, T), lambda i, here: (i, here[3])),
                pl.BlockSpec((per * T, T), lambda i, here: (i, 1 - here[3])),
                WHOLE,
            ],
            out_specs=[pl.BlockSpec((per, T, T), lambda i, here: (i, 0, 0))] * 2,
        ),
        compiler_params=pltpu.CompilerParams(vmem_limit_bytes=8 << 20),
        name="turn_rows",
    )(here, features, features, row_scale)


def slot_of(table, slot):
    row = table[SLOTS + slot]
    block = jnp.where(table[slot] > 0, table[2 * SLOTS + slot], -1)
    return row, block


def forward_body(dys, here, own, sib, st0, st1, *refs):
    count = len(dys)
    z = here[0]
    for g in range(count):
        y_to = lax.rem(here[1] + dys[g], NY)
        inc0, inc1 = refs[2 * g], refs[2 * g + 1]
        for h in range(2):
            out = refs[2 * count + 2 * g + h]

            def one(i, carry, y_to=y_to, inc0=inc0, inc1=inc1, h=h, out=out):
                z_to = lax.rem(z + h * (NZ // 2) + i, NZ)
                for c in range(NC):
                    slot = (z_to * NY + y_to) * NC + c
                    row0, k0 = slot_of(own, slot)
                    row1, k1 = slot_of(sib, slot)
                    a0 = st0[row0]
                    a1 = st1[row1]
                    t0 = inc0[z_to, 0, c]
                    t1 = inc1[z_to, 0, c]
                    zero = jnp.zeros_like(t0)
                    left = jnp.concatenate([a0, a1], axis=1)
                    columns = [
                        jnp.concatenate(
                            [jnp.where(k0 == b, t0, zero), jnp.where(k1 == b, t1, zero)], axis=0
                        )
                        for b in range(2)
                    ]
                    right = jnp.concatenate(columns, axis=1)
                    got = jnp.dot(left, right, preferred_element_type=F32).astype(out.dtype)
                    out[i, 2 * c] = got[:, :T]
                    out[i, 2 * c + 1] = got[:, T:]
                return carry

            lax.fori_loop(0, NZ // 2, one, 0, unroll=4)


def forward(dys, dtype, tables, st, inc0, inc1):
    specs = [WHOLE] * len(st)
    args = [*st]
    for dy in dys:
        for inc in (inc0, inc1):
            specs.append(tile_spec(dy))
            args.append(inc)
    half = (NZ // 2, 2 * NC, T, T)
    return pl.pallas_call(
        functools.partial(forward_body, dys),
        out_shape=[jax.ShapeDtypeStruct(half, dtype)] * (2 * len(dys)),
        grid_spec=pltpu.PrefetchScalarGridSpec(
            num_scalar_prefetch=3,
            grid=(1,),
            in_specs=specs,
            out_specs=[WHOLE] * (2 * len(dys)),
        ),
        compiler_params=pltpu.CompilerParams(vmem_limit_bytes=VMEM),
        name="tiles_forward",
    )(*tables, *args)


def tile_spec(dy):
    return pl.BlockSpec(
        (NZ, 1, NC, T, T), lambda i, here, own, sib: (0, lax.rem(here[1] + dy, NY), 0, 0, 0)
    )


def backward_body(dys, first, share, here, own, sib, *refs):
    refs = list(refs)
    before = None if first else refs.pop(0)
    groups = [[refs.pop(0) for _ in range(4)] for _ in dys]
    total = refs.pop()
    if first:
        total[...] = jnp.zeros_like(total)
    else:
        total[...] = before[...]
    z = here[0]
    for dy, (inc0, inc1, *halves) in zip(dys, groups):
        y_to = lax.rem(here[1] + dy, NY)
        for h, held in enumerate(halves):

            def one(i, carry, y_to=y_to, inc=(inc0, inc1), h=h, held=held):
                z_to = lax.rem(z + h * (NZ // 2) + i, NZ)
                sums = []
                for c in range(NC):
                    slot = (z_to * NY + y_to) * NC + c
                    for s in range(2):
                        row, k = slot_of((own, sib)[s], slot)
                        if share:
                            turn = lax.rem(row // 4 - here[2] + NX, NX)
                            row = turn * 8 + s * 4 + lax.rem(row, 4)
                        else:
                            row = s * 16 + row
                        block = held[i, 2 * c + jnp.maximum(k, 0)]
                        block = jnp.where(k >= 0, block, jnp.zeros_like(block))
                        got = lax.dot_general(
                            block,
                            inc[s][z_to, 0, c],
                            (((1,), (1,)), ((), ())),
                            preferred_element_type=F32,
                        )
                        sums.append((row, got))
                for row, got in sums:
                    total[row] += got
                return carry

            lax.fori_loop(0, NZ // 2, one, 0, unroll=4)
    start = 0
    for out in refs:
        size = out.shape[0]
        out[...] = total[pl.ds(start, size)].astype(out.dtype)
        start += size


def backward(dys, before, outs, share, tables, inc0, inc1, helds):
    first = before is None
    blocks = 2 * 16
    specs = [] if first else [WHOLE]
    args = [] if first else [before]
    for g in range(len(dys)):
        for inc in (inc0, inc1):
            specs.append(tile_spec(dys[g]))
            args.append(inc)
        for held in helds[g]:
            specs.append(WHOLE)
            args.append(held)
    if outs:
        shapes = [jax.ShapeDtypeStruct((n, T, T), dtype) for n, dtype in outs]
        out_specs = [WHOLE] * len(shapes)
        scratch = [pltpu.VMEM((blocks, T, T), F32)]
    else:
        shapes = jax.ShapeDtypeStruct((blocks, T, T), F32)
        out_specs = WHOLE
        scratch = []
    return pl.pallas_call(
        functools.partial(backward_body, dys, first, share),
        out_shape=shapes,
        grid_spec=pltpu.PrefetchScalarGridSpec(
            num_scalar_prefetch=3,
            grid=(1,),
            in_specs=specs,
            out_specs=out_specs,
            scratch_shapes=scratch,
        ),
        compiler_params=pltpu.CompilerParams(vmem_limit_bytes=VMEM),
        name="tiles_backward",
    )(*tables, *args)


def over(a):
    return lax.broadcast_in_dim(a, (a.shape[0], T, T), (0, 2))


def plus(a, b):
    return (a.astype(F32) + b.astype(F32)).astype(BF)


def shards(
    features, incidence, send_count, row_block, edge_block, edge_weight, edge_degree, vertex_degree
):
    vert = lax.axis_index("vert")
    x = lax.axis_index("edge")
    z, y, c = vert // (NY * NC), (vert // NC) % NY, vert % NC
    rows = features.shape[0]
    blocks = rows // T
    per = blocks // NX

    here = jnp.stack([z, y, x, c]).astype(jnp.int32)
    degree = vertex_degree.reshape(blocks, T)
    row_scale = 1.0 / jnp.sqrt(jnp.maximum(degree, 1).astype(F32))
    hyper_scale = edge_weight / jnp.maximum(edge_degree, 1).astype(F32)
    first = c == 0
    begin = x * per
    here, first, begin, row_scale, features = lax.optimization_barrier(
        (here, first, begin, row_scale, features)
    )
    inc0 = incidence.reshape(NZ, NY, NC, T, T)
    inc1 = to_sibling(incidence).reshape(NZ, NY, NC, T, T)
    kept, sent = turned(features, row_scale, here)
    st = (kept, to_sibling(sent))
    own = jnp.concatenate([send_count[:, 0], row_block[:, 0], edge_block[:, 0]])
    tables = (here, own, to_sibling(own))
    scales = to_sibling(jnp.concatenate([row_scale, hyper_scale]))
    scale = (row_scale, scales[:blocks])
    there = scales[blocks:]
    hs = jnp.concatenate(
        [jnp.where(first, hyper_scale, there), jnp.where(first, there, hyper_scale)]
    )
    own_scale = jnp.concatenate([lax.dynamic_slice_in_dim(r, begin, per) for r in scale])
    tables, hs, own_scale = lax.optimization_barrier((tables, hs, own_scale))
    hs, own_scale = over(hs), over(own_scale)

    for applied in range(2):
        a2, b2 = forward((2,), BF, tables, st, inc0, inc1)
        a2, b2 = along_y(a2, 1), along_y(b2, -1)
        a1, b1, a3, b3 = forward((1, 3), BF, tables, st, inc0, inc1)
        up_b, down_a = along_y(b1, 1), along_y(a3, -1)
        a0, b0 = forward((0,), F32, tables, st, inc0, inc1)
        up_a, down_b = along_y(plus(a1, a2), 1), along_y(plus(b3, b2), -1)
        a = a0 + up_a.astype(F32) + down_a.astype(F32)
        b = b0 + up_b.astype(F32) + down_b.astype(F32)
        near_up = jnp.stack([a[3], a[1]]).astype(BF)
        near_down = jnp.stack([b[1], b[3]]).astype(BF)
        near_up, near_down = along_z(near_up, 1), along_z(near_down, -1)
        far_up, far_down = along_z(b[0, :NC].astype(BF), 2), along_z(b[0, NC:].astype(BF), -2)
        near_up, near_down = near_up.astype(F32), near_down.astype(F32)
        far_up = jnp.pad(far_up.astype(F32), ((0, NC), (0, 0), (0, 0)))
        far_down = jnp.pad(far_down.astype(F32), ((NC, 0), (0, 0), (0, 0)))
        up = along_z((a[2] + near_up[0] + far_up).astype(BF), 2)
        down = along_z((b[2] + near_down[0] + far_down).astype(BF), -2)
        hyper_sum = a[0] + near_up[1] + near_down[1] + up.astype(F32) + down.astype(F32)
        hyper = (hs * hyper_sum).astype(BF)

        up2, down2 = along_z(hyper, 2), along_z(hyper, -2)
        up = along_z(jnp.stack([hyper, up2]), 1)
        down = along_z(jnp.stack([hyper, down2]), -1)
        across = jnp.concatenate([along_z(up2[:NC], 2), along_z(down2[NC:], -2)])
        here_a = jnp.stack([hyper, down[0], down2, down[1]])
        up_a, down_a = along_y(here_a, 1), along_y(here_a, -1)
        here_b = jnp.stack([across, up[1], up2, up[0]])
        up_b, down_b = along_y(here_b, 1), along_y(here_b, -1)
        total = backward((0,), None, None, applied == 1, tables, inc0, inc1, ((here_a, here_b),))
        up_a, down_b, total = lax.optimization_barrier((up_a, down_b, total))
        far_a, far_b = along_y(up_a, 1), along_y(down_b, -1)
        total = backward(
            (3, 1),
            total,
            None,
            applied == 1,
            tables,
            inc0,
            inc1,
            ((up_a, up_b), (down_a, down_b)),
        )
        if applied == 0:
            outs = [(blocks, BF)] * 2
        else:
            outs = [(2 * per, F32)] + [(per, BF)] * (2 * (NX - 1))
        parts = backward((2,), total, outs, applied == 1, tables, inc0, inc1, ((far_a, far_b),))
        if applied == 0:
            p, q = parts
            up_p, down_q = along_x(p, 1), along_x(q, -1)
            up_q, down_p = along_x(q, 1), along_x(p, -1)
            far_p, far_q = along_x(up_p, 1), along_x(down_q, -1)
            st = tuple(
                (over(r) * (over(r) * sum(n.astype(F32) for n in group))).astype(BF)
                for r, group in zip(scale, ((p, up_p, down_p, far_p), (q, up_q, down_q, far_q)))
            )
    own, p1, q1, p2, q2, p3, q3 = parts
    p2, q2 = along_x(p2, 1), along_x(q2, -1)
    up_q, down_p = along_x(q1, 1), along_x(p3, -1)
    up_p, down_q = along_x(plus(p1, p2), 1), along_x(plus(q3, q2), -1)
    up = jnp.concatenate([up_p, up_q]).astype(F32)
    down = jnp.concatenate([down_p, down_q]).astype(F32)
    current = own_scale * (own + up + down)
    kept, came = current[:per], to_sibling(current[per:])
    pair = jnp.stack([jnp.where(first, kept, came), jnp.where(first, came, kept)])
    return pair.transpose(1, 3, 0, 2).reshape(per * T, NC * T)


def solution(mesh):
    placed = (
        P("vert", None),
        P("vert", None, "edge"),
        P("vert", "edge"),
        P("vert", "edge"),
        P("vert", "edge"),
        P("vert", "edge"),
        P("vert", "edge"),
        P("vert"),
    )
    return jax.shard_map(
        shards, mesh=mesh, in_specs=placed, out_specs=P(("vert", "edge"), None), check_vma=False
    )
```

```python
import functools

import jax
import jax.numpy as jnp
from jax import lax
from jax.experimental import pallas as pl
from jax.experimental.pallas import tpu as pltpu
from jax.sharding import PartitionSpec as P


NZ, NY, NC, NX = 8, 4, 2, 4
T = 128
SLOTS = NZ * NY * NC
VMEM = 16 << 20
WHOLE = pl.BlockSpec(memory_space=pltpu.VMEM)
BF = jnp.bfloat16
F32 = jnp.float32


def moved(dz, dy, flip):
    pairs = []
    for z in range(NZ):
        for y in range(NY):
            for c in range(NC):
                here = (z * NY + y) * NC + c
                there = (((z + dz) % NZ) * NY + (y + dy) % NY) * NC + (c ^ flip)
                pairs.append((here, there))
    return pairs


def along_z(a, step):
    return lax.ppermute(a, "vert", moved(step, 0, 0))


def to_sibling(a):
    return lax.ppermute(a, "vert", moved(0, 0, 1))


def each_way(dz, dy, dx):
    pairs = []
    for z in range(NZ):
        for y in range(NY):
            for c in range(NC):
                way = 1 - 2 * c
                here = (z * NY + y) * NC + c
                there = (((z + way * dz) % NZ) * NY + (y + way * dy) % NY) * NC + c
                for x in range(NX):
                    pairs.append((here * NX + x, there * NX + (x + way * dx) % NX))
    return pairs


def along_z_each(a, step):
    return lax.ppermute(a, ("vert", "edge"), each_way(step, 0, 0))


def along_y_each(a, step):
    return lax.ppermute(a, ("vert", "edge"), each_way(0, step, 0))


def along_x_each(a, step):
    return lax.ppermute(a, ("vert", "edge"), each_way(0, 0, step))


def turn_body(per, here, kept_in, sent_in, scale, kept, sent):
    for r in range(per):
        rows = pl.ds(r * T, T)
        by = scale[pl.ds(pl.program_id(0) * per + r, 1)]
        kept[r] = (kept_in[rows].T * by).astype(BF)
        sent[r] = (sent_in[rows].T * by).astype(BF)


def turned(features, row_scale, here):
    blocks = features.shape[0] // T
    per = 4
    return pl.pallas_call(
        functools.partial(turn_body, per),
        out_shape=[jax.ShapeDtypeStruct((blocks, T, T), BF)] * 2,
        grid_spec=pltpu.PrefetchScalarGridSpec(
            num_scalar_prefetch=1,
            grid=(blocks // per,),
            in_specs=[
                pl.BlockSpec((per * T, T), lambda i, here: (i, here[3])),
                pl.BlockSpec((per * T, T), lambda i, here: (i, 1 - here[3])),
                WHOLE,
            ],
            out_specs=[pl.BlockSpec((per, T, T), lambda i, here: (i, 0, 0))] * 2,
        ),
        compiler_params=pltpu.CompilerParams(vmem_limit_bytes=8 << 20),
        name="turn_rows",
    )(here, features, features, row_scale)


WAY, BACK = 4, 5


def owner_y(here, dy):
    return lax.rem(here[1] + (dy if dy < WAY else here[dy]), NY)


def slot_of(table, slot):
    row = table[SLOTS + slot]
    block = jnp.where(table[slot] > 0, table[2 * SLOTS + slot], -1)
    return row, block


def forward_body(dys, here, own, sib, st0, st1, *refs):
    count = len(dys)
    z = here[0]
    for g in range(count):
        y_to = owner_y(here, dys[g])
        inc0, inc1 = refs[2 * g], refs[2 * g + 1]
        out = refs[2 * count + g]

        def one(i, carry, y_to=y_to, inc0=inc0, inc1=inc1, out=out):
            z_to = lax.rem(z + i, NZ)
            for c in range(NC):
                slot = (z_to * NY + y_to) * NC + c
                row0, k0 = slot_of(own, slot)
                row1, k1 = slot_of(sib, slot)
                a0 = st0[row0]
                a1 = st1[row1]
                t0 = inc0[z_to, 0, c]
                t1 = inc1[z_to, 0, c]
                zero = jnp.zeros_like(t0)
                left = jnp.concatenate([a0, a1], axis=1)
                columns = [
                    jnp.concatenate(
                        [jnp.where(k0 == b, t0, zero), jnp.where(k1 == b, t1, zero)], axis=0
                    )
                    for b in range(2)
                ]
                right = jnp.concatenate(columns, axis=1)
                got = jnp.dot(left, right, preferred_element_type=F32).astype(out.dtype)
                out[i, 2 * c] = got[:, :T]
                out[i, 2 * c + 1] = got[:, T:]
            return carry

        lax.fori_loop(0, NZ, one, 0, unroll=4)


def forward(dys, dtype, tables, st, inc0, inc1):
    specs = [WHOLE] * len(st)
    args = [*st]
    for dy in dys:
        for inc in (inc0, inc1):
            specs.append(tile_spec(dy))
            args.append(inc)
    whole = (NZ, 2 * NC, T, T)
    return pl.pallas_call(
        functools.partial(forward_body, dys),
        out_shape=[jax.ShapeDtypeStruct(whole, dtype)] * len(dys),
        grid_spec=pltpu.PrefetchScalarGridSpec(
            num_scalar_prefetch=3,
            grid=(1,),
            in_specs=specs,
            out_specs=[WHOLE] * len(dys),
        ),
        compiler_params=pltpu.CompilerParams(vmem_limit_bytes=VMEM),
        name="tiles_forward",
    )(*tables, *args)


def tile_spec(dy):
    return pl.BlockSpec(
        (NZ, 1, NC, T, T), lambda i, here, own, sib: (0, owner_y(here, dy), 0, 0, 0)
    )


def backward_body(dys, first, share, here, own, sib, *refs):
    refs = list(refs)
    before = None if first else refs.pop(0)
    groups = [[refs.pop(0) for _ in range(3)] for _ in dys]
    total = refs.pop()
    if first:
        total[...] = jnp.zeros_like(total)
    else:
        total[...] = before[...]
    z = here[0]
    for dy, (inc0, inc1, held) in zip(dys, groups):
        y_to = owner_y(here, dy)

        def one(i, carry, y_to=y_to, inc=(inc0, inc1), held=held):
            z_to = lax.rem(z + i, NZ)
            sums = []
            for c in range(NC):
                slot = (z_to * NY + y_to) * NC + c
                for s in range(2):
                    row, k = slot_of((own, sib)[s], slot)
                    if share:
                        turn = lax.rem((row // 4 - here[2] + NX) * here[WAY], NX)
                        row = turn * 8 + s * 4 + lax.rem(row, 4)
                    else:
                        row = s * 16 + row
                    block = held[i, 2 * c + jnp.maximum(k, 0)]
                    block = jnp.where(k >= 0, block, jnp.zeros_like(block))
                    got = lax.dot_general(
                        block,
                        inc[s][z_to, 0, c],
                        (((1,), (1,)), ((), ())),
                        preferred_element_type=F32,
                    )
                    sums.append((row, got))
            for row, got in sums:
                total[row] += got
            return carry

        lax.fori_loop(0, NZ, one, 0, unroll=4)
    start = 0
    for out in refs:
        size = out.shape[0]
        out[...] = total[pl.ds(start, size)].astype(out.dtype)
        start += size


def backward(dys, before, outs, share, tables, inc0, inc1, helds):
    first = before is None
    blocks = 2 * 16
    specs = [] if first else [WHOLE]
    args = [] if first else [before]
    for g in range(len(dys)):
        for inc in (inc0, inc1):
            specs.append(tile_spec(dys[g]))
            args.append(inc)
        specs.append(WHOLE)
        args.append(helds[g])
    if outs:
        shapes = [jax.ShapeDtypeStruct((n, T, T), dtype) for n, dtype in outs]
        out_specs = [WHOLE] * len(shapes)
        scratch = [pltpu.VMEM((blocks, T, T), F32)]
    else:
        shapes = jax.ShapeDtypeStruct((blocks, T, T), F32)
        out_specs = WHOLE
        scratch = []
    return pl.pallas_call(
        functools.partial(backward_body, dys, first, share),
        out_shape=shapes,
        grid_spec=pltpu.PrefetchScalarGridSpec(
            num_scalar_prefetch=3,
            grid=(1,),
            in_specs=specs,
            out_specs=out_specs,
            scratch_shapes=scratch,
        ),
        compiler_params=pltpu.CompilerParams(vmem_limit_bytes=VMEM),
        name="tiles_backward",
    )(*tables, *args)


def over(a):
    return lax.broadcast_in_dim(a, (a.shape[0], T, T), (0, 2))


def plus(a, b):
    return (a.astype(F32) + b.astype(F32)).astype(BF)


def shards(
    features, incidence, send_count, row_block, edge_block, edge_weight, edge_degree, vertex_degree
):
    vert = lax.axis_index("vert")
    x = lax.axis_index("edge")
    z, y, c = vert // (NY * NC), (vert // NC) % NY, vert % NC
    rows = features.shape[0]
    blocks = rows // T
    per = blocks // NX

    here = jnp.stack([z, y, x, c, 1 + 2 * c, 3 - 2 * c]).astype(jnp.int32)
    degree = vertex_degree.reshape(blocks, T)
    row_scale = 1.0 / jnp.sqrt(jnp.maximum(degree, 1).astype(F32))
    hyper_scale = edge_weight / jnp.maximum(edge_degree, 1).astype(F32)
    first = c == 0
    begin = x * per
    here, first, begin, row_scale, features = lax.optimization_barrier(
        (here, first, begin, row_scale, features)
    )
    inc0 = incidence.reshape(NZ, NY, NC, T, T)
    inc1 = to_sibling(incidence).reshape(NZ, NY, NC, T, T)
    kept, sent = turned(features, row_scale, here)
    st = (kept, to_sibling(sent))
    own = jnp.concatenate([send_count[:, 0], row_block[:, 0], edge_block[:, 0]])
    tables = (here, own, to_sibling(own))
    scales = to_sibling(jnp.concatenate([row_scale, hyper_scale]))
    scale = (row_scale, scales[:blocks])
    there = scales[blocks:]
    hs = jnp.concatenate(
        [jnp.where(first, hyper_scale, there), jnp.where(first, there, hyper_scale)]
    )
    own_scale = jnp.concatenate([lax.dynamic_slice_in_dim(r, begin, per) for r in scale])
    tables, hs, own_scale = lax.optimization_barrier((tables, hs, own_scale))
    hs, own_scale = over(hs), over(own_scale)

    for applied in range(2):
        (far,) = forward((2,), BF, tables, st, inc0, inc1)
        far = along_y_each(far, 1)
        way, back = forward((WAY, BACK), BF, tables, st, inc0, inc1)
        back = along_y_each(back, -1)
        (level,) = forward((0,), F32, tables, st, inc0, inc1)
        way = along_y_each(plus(way, far), 1)
        s = level + back.astype(F32) + way.astype(F32)
        near_up = along_z(jnp.stack([s[3], s[1]]).astype(BF), 1).astype(F32)
        near_down = along_z(jnp.stack([s[5], s[7]]).astype(BF), -1).astype(F32)
        far = along_z_each(s[4].astype(BF), 2).astype(F32)
        zero = jnp.zeros_like(far)
        up = along_z((s[2] + near_up[0] + jnp.where(first, far, zero)).astype(BF), 2)
        down = along_z((s[6] + near_down[0] + jnp.where(first, zero, far)).astype(BF), -2)
        hyper_sum = s[0] + near_up[1] + near_down[1] + up.astype(F32) + down.astype(F32)
        hyper = (hs * hyper_sum).astype(BF)

        up2, down2 = along_z(hyper, 2), along_z(hyper, -2)
        up = along_z(jnp.stack([hyper, up2]), 1)
        down = along_z(jnp.stack([hyper, down2]), -1)
        across = along_z_each(jnp.where(first, up2, down2), 2)
        level = jnp.stack([hyper, down[0], down2, down[1], across, up[1], up2, up[0]])
        back, way = along_y_each(level, 1), along_y_each(level, -1)
        share = applied == 1
        total = backward((0,), None, None, share, tables, inc0, inc1, (level,))
        back, total = lax.optimization_barrier((back, total))
        far = along_y_each(back, 1)
        total = backward((BACK, WAY), total, None, share, tables, inc0, inc1, (back, way))
        if share:
            outs = [(2 * per, F32)] + [(2 * per, BF)] * (NX - 1)
        else:
            outs = [(2 * blocks, BF)]
        parts = backward((2,), total, outs, share, tables, inc0, inc1, (far,))
        if not share:
            (own,) = parts
            back, way = along_x_each(own, 1), along_x_each(own, -1)
            far = along_x_each(back, 1)
            st = tuple(
                (
                    over(r)
                    * (over(r) * sum(n[at : at + blocks].astype(F32) for n in (own, back, way, far)))
                ).astype(BF)
                for r, at in zip(scale, (0, blocks))
            )
    own, way, far, back = parts
    far, back = along_x_each(far, 1), along_x_each(back, -1)
    way = along_x_each(plus(way, far), 1)
    current = own_scale * (own + back.astype(F32) + way.astype(F32))
    kept, came = current[:per], to_sibling(current[per:])
    pair = jnp.stack([jnp.where(first, kept, came), jnp.where(first, came, kept)])
    return pair.transpose(1, 3, 0, 2).reshape(per * T, NC * T)


def solution(mesh):
    placed = (
        P("vert", None),
        P("vert", None, "edge"),
        P("vert", "edge"),
        P("vert", "edge"),
        P("vert", "edge"),
        P("vert", "edge"),
        P("vert", "edge"),
        P("vert"),
    )
    return jax.shard_map(
        shards, mesh=mesh, in_specs=placed, out_specs=P(("vert", "edge"), None), check_vma=False
    )
```

```python
import functools

import jax
import jax.numpy as jnp
from jax import lax
from jax.experimental import pallas as pl
from jax.experimental.pallas import tpu as pltpu
from jax.sharding import PartitionSpec as P


NZ, NY, NC, NX = 8, 4, 2, 4
T = 128
SLOTS = NZ * NY * NC
VMEM = 16 << 20
WHOLE = pl.BlockSpec(memory_space=pltpu.VMEM)
BF = jnp.bfloat16
F32 = jnp.float32


def moved(dz, dy, flip):
    pairs = []
    for z in range(NZ):
        for y in range(NY):
            for c in range(NC):
                here = (z * NY + y) * NC + c
                there = (((z + dz) % NZ) * NY + (y + dy) % NY) * NC + (c ^ flip)
                pairs.append((here, there))
    return pairs


def along_z(a, step):
    return lax.ppermute(a, "vert", moved(step, 0, 0))


def along_y(a, step):
    return lax.ppermute(a, "vert", moved(0, step, 0))


def to_sibling(a):
    return lax.ppermute(a, "vert", moved(0, 0, 1))


def along_x(a, step):
    return lax.ppermute(a, "edge", [(i, (i + step) % NX) for i in range(NX)])


def along_z_each(a, step):
    pairs = moved(step, 0, 0)
    back = moved(-step, 0, 0)
    return lax.ppermute(a, "vert", [(back if p[0] % NC else pairs)[n] for n, p in enumerate(pairs)])


def turn_body(per, here, kept_in, sent_in, scale, kept, sent):
    for r in range(per):
        rows = pl.ds(r * T, T)
        by = scale[pl.ds(pl.program_id(0) * per + r, 1)]
        kept[r] = (kept_in[rows].T * by).astype(BF)
        sent[r] = (sent_in[rows].T * by).astype(BF)


def turned(features, row_scale, here):
    blocks = features.shape[0] // T
    per = 4
    return pl.pallas_call(
        functools.partial(turn_body, per),
        out_shape=[jax.ShapeDtypeStruct((blocks, T, T), BF)] * 2,
        grid_spec=pltpu.PrefetchScalarGridSpec(
            num_scalar_prefetch=1,
            grid=(blocks // per,),
            in_specs=[
                pl.BlockSpec((per * T, T), lambda i, here: (i, here[3])),
                pl.BlockSpec((per * T, T), lambda i, here: (i, 1 - here[3])),
                WHOLE,
            ],
            out_specs=[pl.BlockSpec((per, T, T), lambda i, here: (i, 0, 0))] * 2,
        ),
        compiler_params=pltpu.CompilerParams(vmem_limit_bytes=8 << 20),
        name="turn_rows",
    )(here, features, features, row_scale)


def slot_of(table, slot):
    row = table[SLOTS + slot]
    block = jnp.where(table[slot] > 0, table[2 * SLOTS + slot], -1)
    return row, block


def forward_body(dys, here, own, sib, st0, st1, *refs):
    count = len(dys)
    z = here[0]
    for g in range(count):
        y_to = lax.rem(here[1] + dys[g], NY)
        inc0, inc1 = refs[2 * g], refs[2 * g + 1]
        for h in range(2):
            out = refs[2 * count + 2 * g + h]

            def one(i, carry, y_to=y_to, inc0=inc0, inc1=inc1, h=h, out=out):
                z_to = lax.rem(z + h * (NZ // 2) + i, NZ)
                for c in range(NC):
                    slot = (z_to * NY + y_to) * NC + c
                    row0, k0 = slot_of(own, slot)
                    row1, k1 = slot_of(sib, slot)
                    a0 = st0[row0]
                    a1 = st1[row1]
                    t0 = inc0[z_to, 0, c]
                    t1 = inc1[z_to, 0, c]
                    zero = jnp.zeros_like(t0)
                    left = jnp.concatenate([a0, a1], axis=1)
                    columns = [
                        jnp.concatenate(
                            [jnp.where(k0 == b, t0, zero), jnp.where(k1 == b, t1, zero)], axis=0
                        )
                        for b in range(2)
                    ]
                    right = jnp.concatenate(columns, axis=1)
                    got = jnp.dot(left, right, preferred_element_type=F32).astype(out.dtype)
                    out[i, 2 * c] = got[:, :T]
                    out[i, 2 * c + 1] = got[:, T:]
                return carry

            lax.fori_loop(0, NZ // 2, one, 0, unroll=4)


def forward(dys, dtype, tables, st, inc0, inc1):
    specs = [WHOLE] * len(st)
    args = [*st]
    for dy in dys:
        for inc in (inc0, inc1):
            specs.append(tile_spec(dy))
            args.append(inc)
    half = (NZ // 2, 2 * NC, T, T)
    return pl.pallas_call(
        functools.partial(forward_body, dys),
        out_shape=[jax.ShapeDtypeStruct(half, dtype)] * (2 * len(dys)),
        grid_spec=pltpu.PrefetchScalarGridSpec(
            num_scalar_prefetch=3,
            grid=(1,),
            in_specs=specs,
            out_specs=[WHOLE] * (2 * len(dys)),
        ),
        compiler_params=pltpu.CompilerParams(vmem_limit_bytes=VMEM),
        name="tiles_forward",
    )(*tables, *args)


def tile_spec(dy):
    return pl.BlockSpec(
        (NZ, 1, NC, T, T), lambda i, here, own, sib: (0, lax.rem(here[1] + dy, NY), 0, 0, 0)
    )


def backward_body(dys, first, share, here, own, sib, *refs):
    refs = list(refs)
    before = None if first else refs.pop(0)
    groups = [[refs.pop(0) for _ in range(4)] for _ in dys]
    total = refs.pop()
    if first:
        total[...] = jnp.zeros_like(total)
    else:
        total[...] = before[...]
    z = here[0]
    for dy, (inc0, inc1, *halves) in zip(dys, groups):
        y_to = lax.rem(here[1] + dy, NY)
        for h, held in enumerate(halves):

            def one(i, carry, y_to=y_to, inc=(inc0, inc1), h=h, held=held):
                z_to = lax.rem(z + h * (NZ // 2) + i, NZ)
                sums = []
                for c in range(NC):
                    slot = (z_to * NY + y_to) * NC + c
                    for s in range(2):
                        row, k = slot_of((own, sib)[s], slot)
                        if share:
                            turn = lax.rem(row // 4 - here[2] + NX, NX)
                            row = turn * 8 + s * 4 + lax.rem(row, 4)
                        else:
                            row = s * 16 + row
                        block = held[i, 2 * c + jnp.maximum(k, 0)]
                        block = jnp.where(k >= 0, block, jnp.zeros_like(block))
                        got = lax.dot_general(
                            block,
                            inc[s][z_to, 0, c],
                            (((1,), (1,)), ((), ())),
                            preferred_element_type=F32,
                        )
                        sums.append((row, got))
                for row, got in sums:
                    total[row] += got
                return carry

            lax.fori_loop(0, NZ // 2, one, 0, unroll=4)
    start = 0
    for out in refs:
        size = out.shape[0]
        out[...] = total[pl.ds(start, size)].astype(out.dtype)
        start += size


def backward(dys, before, outs, share, tables, inc0, inc1, helds):
    first = before is None
    blocks = 2 * 16
    specs = [] if first else [WHOLE]
    args = [] if first else [before]
    for g in range(len(dys)):
        for inc in (inc0, inc1):
            specs.append(tile_spec(dys[g]))
            args.append(inc)
        for held in helds[g]:
            specs.append(WHOLE)
            args.append(held)
    if outs:
        shapes = [jax.ShapeDtypeStruct((n, T, T), dtype) for n, dtype in outs]
        out_specs = [WHOLE] * len(shapes)
        scratch = [pltpu.VMEM((blocks, T, T), F32)]
    else:
        shapes = jax.ShapeDtypeStruct((blocks, T, T), F32)
        out_specs = WHOLE
        scratch = []
    return pl.pallas_call(
        functools.partial(backward_body, dys, first, share),
        out_shape=shapes,
        grid_spec=pltpu.PrefetchScalarGridSpec(
            num_scalar_prefetch=3,
            grid=(1,),
            in_specs=specs,
            out_specs=out_specs,
            scratch_shapes=scratch,
        ),
        compiler_params=pltpu.CompilerParams(vmem_limit_bytes=VMEM),
        name="tiles_backward",
    )(*tables, *args)


def over(a):
    return lax.broadcast_in_dim(a, (a.shape[0], T, T), (0, 2))


def plus(a, b):
    return (a.astype(F32) + b.astype(F32)).astype(BF)


def shards(
    features, incidence, send_count, row_block, edge_block, edge_weight, edge_degree, vertex_degree
):
    vert = lax.axis_index("vert")
    x = lax.axis_index("edge")
    z, y, c = vert // (NY * NC), (vert // NC) % NY, vert % NC
    rows = features.shape[0]
    blocks = rows // T
    per = blocks // NX

    here = jnp.stack([z, y, x, c]).astype(jnp.int32)
    degree = vertex_degree.reshape(blocks, T)
    row_scale = 1.0 / jnp.sqrt(jnp.maximum(degree, 1).astype(F32))
    hyper_scale = edge_weight / jnp.maximum(edge_degree, 1).astype(F32)
    first = c == 0
    begin = x * per
    here, first, begin, row_scale, features = lax.optimization_barrier(
        (here, first, begin, row_scale, features)
    )
    inc0 = incidence.reshape(NZ, NY, NC, T, T)
    inc1 = to_sibling(incidence).reshape(NZ, NY, NC, T, T)
    kept, sent = turned(features, row_scale, here)
    st = (kept, to_sibling(sent))
    own = jnp.concatenate([send_count[:, 0], row_block[:, 0], edge_block[:, 0]])
    tables = (here, own, to_sibling(own))
    scales = to_sibling(jnp.concatenate([row_scale, hyper_scale]))
    scale = (row_scale, scales[:blocks])
    there = scales[blocks:]
    hs = jnp.concatenate(
        [jnp.where(first, hyper_scale, there), jnp.where(first, there, hyper_scale)]
    )
    own_scale = jnp.concatenate([lax.dynamic_slice_in_dim(r, begin, per) for r in scale])
    tables, hs, own_scale = lax.optimization_barrier((tables, hs, own_scale))
    hs, own_scale = over(hs), over(own_scale)

    for applied in range(2):
        a2, b2 = forward((2,), BF, tables, st, inc0, inc1)
        a2, b2 = along_y(a2, 1), along_y(b2, -1)
        a1, b1, a3, b3 = forward((1, 3), BF, tables, st, inc0, inc1)
        up_b, down_a = along_y(b1, 1), along_y(a3, -1)
        a0, b0 = forward((0,), F32, tables, st, inc0, inc1)
        up_a, down_b = along_y(plus(a1, a2), 1), along_y(plus(b3, b2), -1)
        a = a0 + up_a.astype(F32) + down_a.astype(F32)
        b = b0 + up_b.astype(F32) + down_b.astype(F32)
        near_up = jnp.stack([a[3], a[1]]).astype(BF)
        near_down = jnp.stack([b[1], b[3]]).astype(BF)
        near_up, near_down = along_z(near_up, 1), along_z(near_down, -1)
        far = along_z_each(b[0].astype(BF), 2).astype(F32)
        near_up, near_down = near_up.astype(F32), near_down.astype(F32)
        zero = jnp.zeros_like(far)
        up = along_z((a[2] + near_up[0] + jnp.where(first, far, zero)).astype(BF), 2)
        down = along_z((b[2] + near_down[0] + jnp.where(first, zero, far)).astype(BF), -2)
        hyper_sum = a[0] + near_up[1] + near_down[1] + up.astype(F32) + down.astype(F32)
        hyper = (hs * hyper_sum).astype(BF)

        up2, down2 = along_z(hyper, 2), along_z(hyper, -2)
        up = along_z(jnp.stack([hyper, up2]), 1)
        down = along_z(jnp.stack([hyper, down2]), -1)
        across = jnp.concatenate([along_z(up2[:NC], 2), along_z(down2[NC:], -2)])
        here_a = jnp.stack([hyper, down[0], down2, down[1]])
        up_a, down_a = along_y(here_a, 1), along_y(here_a, -1)
        here_b = jnp.stack([across, up[1], up2, up[0]])
        up_b, down_b = along_y(here_b, 1), along_y(here_b, -1)
        total = backward((0,), None, None, applied == 1, tables, inc0, inc1, ((here_a, here_b),))
        up_a, down_b, total = lax.optimization_barrier((up_a, down_b, total))
        far_a, far_b = along_y(up_a, 1), along_y(down_b, -1)
        total = backward(
            (3, 1),
            total,
            None,
            applied == 1,
            tables,
            inc0,
            inc1,
            ((up_a, up_b), (down_a, down_b)),
        )
        if applied == 0:
            outs = [(blocks, BF)] * 2
        else:
            outs = [(2 * per, F32)] + [(per, BF)] * (2 * (NX - 1))
        parts = backward((2,), total, outs, applied == 1, tables, inc0, inc1, ((far_a, far_b),))
        if applied == 0:
            p, q = parts
            up_p, down_q = along_x(p, 1), along_x(q, -1)
            up_q, down_p = along_x(q, 1), along_x(p, -1)
            far_p, far_q = along_x(up_p, 1), along_x(down_q, -1)
            st = tuple(
                (over(r) * (over(r) * sum(n.astype(F32) for n in group))).astype(BF)
                for r, group in zip(scale, ((p, up_p, down_p, far_p), (q, up_q, down_q, far_q)))
            )
    own, p1, q1, p2, q2, p3, q3 = parts
    p2, q2 = along_x(p2, 1), along_x(q2, -1)
    up_q, down_p = along_x(q1, 1), along_x(p3, -1)
    up_p, down_q = along_x(plus(p1, p2), 1), along_x(plus(q3, q2), -1)
    up = jnp.concatenate([up_p, up_q]).astype(F32)
    down = jnp.concatenate([down_p, down_q]).astype(F32)
    current = own_scale * (own + up + down)
    kept, came = current[:per], to_sibling(current[per:])
    pair = jnp.stack([jnp.where(first, kept, came), jnp.where(first, came, kept)])
    return pair.transpose(1, 3, 0, 2).reshape(per * T, NC * T)


def solution(mesh):
    placed = (
        P("vert", None),
        P("vert", None, "edge"),
        P("vert", "edge"),
        P("vert", "edge"),
        P("vert", "edge"),
        P("vert", "edge"),
        P("vert", "edge"),
        P("vert"),
    )
    return jax.shard_map(
        shards, mesh=mesh, in_specs=placed, out_specs=P(("vert", "edge"), None), check_vma=False
    )
```

```python
import functools

import jax
import jax.numpy as jnp
from jax import lax
from jax.experimental import pallas as pl
from jax.experimental.pallas import tpu as pltpu
from jax.sharding import PartitionSpec as P


NZ, NY, NC, NX = 8, 4, 2, 4
T = 128
SLOTS = NZ * NY * NC
VMEM = 16 << 20
WHOLE = pl.BlockSpec(memory_space=pltpu.VMEM)
BF = jnp.bfloat16
F32 = jnp.float32


def moved(dz, dy, flip):
    pairs = []
    for z in range(NZ):
        for y in range(NY):
            for c in range(NC):
                here = (z * NY + y) * NC + c
                there = (((z + dz) % NZ) * NY + (y + dy) % NY) * NC + (c ^ flip)
                pairs.append((here, there))
    return pairs


def along_z(a, step):
    return lax.ppermute(a, "vert", moved(step, 0, 0))


def along_y(a, step):
    return lax.ppermute(a, "vert", moved(0, step, 0))


def to_sibling(a):
    return lax.ppermute(a, "vert", moved(0, 0, 1))


def along_x(a, step):
    return lax.ppermute(a, "edge", [(i, (i + step) % NX) for i in range(NX)])


def turn_body(per, here, kept_in, sent_in, scale, kept, sent):
    for r in range(per):
        rows = pl.ds(r * T, T)
        by = scale[pl.ds(pl.program_id(0) * per + r, 1)]
        kept[r] = (kept_in[rows].T * by).astype(BF)
        sent[r] = (sent_in[rows].T * by).astype(BF)


def turned(features, row_scale, here):
    blocks = features.shape[0] // T
    per = 4
    return pl.pallas_call(
        functools.partial(turn_body, per),
        out_shape=[jax.ShapeDtypeStruct((blocks, T, T), BF)] * 2,
        grid_spec=pltpu.PrefetchScalarGridSpec(
            num_scalar_prefetch=1,
            grid=(blocks // per,),
            in_specs=[
                pl.BlockSpec((per * T, T), lambda i, here: (i, here[3])),
                pl.BlockSpec((per * T, T), lambda i, here: (i, 1 - here[3])),
                WHOLE,
            ],
            out_specs=[pl.BlockSpec((per, T, T), lambda i, here: (i, 0, 0))] * 2,
        ),
        compiler_params=pltpu.CompilerParams(vmem_limit_bytes=8 << 20),
        name="turn_rows",
    )(here, features, features, row_scale)


def slot_of(table, slot):
    row = table[SLOTS + slot]
    block = jnp.where(table[slot] > 0, table[2 * SLOTS + slot], -1)
    return row, block


def forward_body(dys, here, own, sib, st0, st1, *refs):
    count = len(dys)
    z = here[0]
    for g in range(count):
        y_to = lax.rem(here[1] + dys[g], NY)
        inc0, inc1 = refs[2 * g], refs[2 * g + 1]
        for h in range(2):
            out = refs[2 * count + 2 * g + h]

            def one(i, carry, y_to=y_to, inc0=inc0, inc1=inc1, h=h, out=out):
                z_to = lax.rem(z + h * (NZ // 2) + i, NZ)
                for c in range(NC):
                    slot = (z_to * NY + y_to) * NC + c
                    row0, k0 = slot_of(own, slot)
                    row1, k1 = slot_of(sib, slot)
                    a0 = st0[row0]
                    a1 = st1[row1]
                    t0 = inc0[z_to, 0, c]
                    t1 = inc1[z_to, 0, c]
                    zero = jnp.zeros_like(t0)
                    left = jnp.concatenate([a0, a1], axis=1)
                    columns = [
                        jnp.concatenate(
                            [jnp.where(k0 == b, t0, zero), jnp.where(k1 == b, t1, zero)], axis=0
                        )
                        for b in range(2)
                    ]
                    right = jnp.concatenate(columns, axis=1)
                    got = jnp.dot(left, right, preferred_element_type=F32).astype(out.dtype)
                    out[i, 2 * c] = got[:, :T]
                    out[i, 2 * c + 1] = got[:, T:]
                return carry

            lax.fori_loop(0, NZ // 2, one, 0, unroll=4)


def forward(dys, dtype, tables, st, inc0, inc1):
    specs = [WHOLE] * len(st)
    args = [*st]
    for dy in dys:
        for inc in (inc0, inc1):
            specs.append(tile_spec(dy))
            args.append(inc)
    half = (NZ // 2, 2 * NC, T, T)
    return pl.pallas_call(
        functools.partial(forward_body, dys),
        out_shape=[jax.ShapeDtypeStruct(half, dtype)] * (2 * len(dys)),
        grid_spec=pltpu.PrefetchScalarGridSpec(
            num_scalar_prefetch=3,
            grid=(1,),
            in_specs=specs,
            out_specs=[WHOLE] * (2 * len(dys)),
        ),
        compiler_params=pltpu.CompilerParams(vmem_limit_bytes=VMEM),
        name="tiles_forward",
    )(*tables, *args)


def tile_spec(dy):
    return pl.BlockSpec(
        (NZ, 1, NC, T, T), lambda i, here, own, sib: (0, lax.rem(here[1] + dy, NY), 0, 0, 0)
    )


def backward_body(dys, first, share, here, own, sib, *refs):
    refs = list(refs)
    before = None if first else refs.pop(0)
    groups = [[refs.pop(0) for _ in range(4)] for _ in dys]
    total = refs.pop()
    if first:
        total[...] = jnp.zeros_like(total)
    else:
        total[...] = before[...]
    z = here[0]
    for dy, (inc0, inc1, *halves) in zip(dys, groups):
        y_to = lax.rem(here[1] + dy, NY)
        for h, held in enumerate(halves):

            def one(i, carry, y_to=y_to, inc=(inc0, inc1), h=h, held=held):
                z_to = lax.rem(z + h * (NZ // 2) + i, NZ)
                sums = []
                for c in range(NC):
                    slot = (z_to * NY + y_to) * NC + c
                    for s in range(2):
                        row, k = slot_of((own, sib)[s], slot)
                        if share:
                            turn = lax.rem(row // 4 - here[2] + NX, NX)
                            row = turn * 8 + s * 4 + lax.rem(row, 4)
                        else:
                            row = s * 16 + row
                        block = held[i, 2 * c + jnp.maximum(k, 0)]
                        block = jnp.where(k >= 0, block, jnp.zeros_like(block))
                        got = lax.dot_general(
                            block,
                            inc[s][z_to, 0, c],
                            (((1,), (1,)), ((), ())),
                            preferred_element_type=F32,
                        )
                        sums.append((row, got))
                for row, got in sums:
                    total[row] += got
                return carry

            lax.fori_loop(0, NZ // 2, one, 0, unroll=4)
    start = 0
    for out in refs:
        size = out.shape[0]
        out[...] = total[pl.ds(start, size)].astype(out.dtype)
        start += size


def backward(dys, before, outs, share, tables, inc0, inc1, helds):
    first = before is None
    blocks = 2 * 16
    specs = [] if first else [WHOLE]
    args = [] if first else [before]
    for g in range(len(dys)):
        for inc in (inc0, inc1):
            specs.append(tile_spec(dys[g]))
            args.append(inc)
        for held in helds[g]:
            specs.append(WHOLE)
            args.append(held)
    if outs:
        shapes = [jax.ShapeDtypeStruct((n, T, T), dtype) for n, dtype in outs]
        out_specs = [WHOLE] * len(shapes)
        scratch = [pltpu.VMEM((blocks, T, T), F32)]
    else:
        shapes = jax.ShapeDtypeStruct((blocks, T, T), F32)
        out_specs = WHOLE
        scratch = []
    return pl.pallas_call(
        functools.partial(backward_body, dys, first, share),
        out_shape=shapes,
        grid_spec=pltpu.PrefetchScalarGridSpec(
            num_scalar_prefetch=3,
            grid=(1,),
            in_specs=specs,
            out_specs=out_specs,
            scratch_shapes=scratch,
        ),
        compiler_params=pltpu.CompilerParams(vmem_limit_bytes=VMEM),
        name="tiles_backward",
    )(*tables, *args)


def over(a):
    return lax.broadcast_in_dim(a, (a.shape[0], T, T), (0, 2))


def plus(a, b):
    return (a.astype(F32) + b.astype(F32)).astype(BF)


def shards(
    features, incidence, send_count, row_block, edge_block, edge_weight, edge_degree, vertex_degree
):
    vert = lax.axis_index("vert")
    x = lax.axis_index("edge")
    z, y, c = vert // (NY * NC), (vert // NC) % NY, vert % NC
    rows = features.shape[0]
    blocks = rows // T
    per = blocks // NX

    here = jnp.stack([z, y, x, c]).astype(jnp.int32)
    degree = vertex_degree.reshape(blocks, T)
    row_scale = 1.0 / jnp.sqrt(jnp.maximum(degree, 1).astype(F32))
    hyper_scale = edge_weight / jnp.maximum(edge_degree, 1).astype(F32)
    first = c == 0
    begin = x * per
    here, first, begin, row_scale, features = lax.optimization_barrier(
        (here, first, begin, row_scale, features)
    )
    inc0 = incidence.reshape(NZ, NY, NC, T, T)
    inc1 = to_sibling(incidence).reshape(NZ, NY, NC, T, T)
    kept, sent = turned(features, row_scale, here)
    st = (kept, to_sibling(sent))
    own = jnp.concatenate([send_count[:, 0], row_block[:, 0], edge_block[:, 0]])
    tables = (here, own, to_sibling(own))
    scales = to_sibling(jnp.concatenate([row_scale, hyper_scale]))
    scale = (row_scale, scales[:blocks])
    there = scales[blocks:]
    hs = jnp.concatenate(
        [jnp.where(first, hyper_scale, there), jnp.where(first, there, hyper_scale)]
    )
    own_scale = jnp.concatenate([lax.dynamic_slice_in_dim(r, begin, per) for r in scale])
    tables, hs, own_scale = lax.optimization_barrier((tables, hs, own_scale))
    hs, own_scale = over(hs), over(own_scale)

    for applied in range(2):
        a2, b2 = forward((2,), BF, tables, st, inc0, inc1)
        a2, b2 = along_y(a2, 1), along_y(b2, -1)
        a1, b1, a3, b3 = forward((1, 3), BF, tables, st, inc0, inc1)
        up_b, down_a = along_y(b1, 1), along_y(a3, -1)
        a0, b0 = forward((0,), F32, tables, st, inc0, inc1)
        up_a, down_b = along_y(plus(a1, a2), 1), along_y(plus(b3, b2), -1)
        a = a0 + up_a.astype(F32) + down_a.astype(F32)
        b = b0 + up_b.astype(F32) + down_b.astype(F32)
        near_up = jnp.stack([a[3], a[1]]).astype(BF)
        near_down = jnp.stack([b[1], b[3]]).astype(BF)
        near_up, near_down = along_z(near_up, 1), along_z(near_down, -1)
        far_up, far_down = along_z(b[0, :NC].astype(BF), 2), along_z(b[0, NC:].astype(BF), -2)
        near_up, near_down = near_up.astype(F32), near_down.astype(F32)
        far_up = jnp.pad(far_up.astype(F32), ((0, NC), (0, 0), (0, 0)))
        far_down = jnp.pad(far_down.astype(F32), ((NC, 0), (0, 0), (0, 0)))
        up = along_z((a[2] + near_up[0] + far_up).astype(BF), 2)
        down = along_z((b[2] + near_down[0] + far_down).astype(BF), -2)
        hyper_sum = a[0] + near_up[1] + near_down[1] + up.astype(F32) + down.astype(F32)
        hyper = (hs * hyper_sum).astype(BF)

        up2, down2 = along_z(hyper, 2), along_z(hyper, -2)
        up = along_z(jnp.stack([hyper, up2]), 1)
        down = along_z(jnp.stack([hyper, down2]), -1)
        across = jnp.concatenate([along_z(up2[:NC], 2), along_z(down2[NC:], -2)])
        here_a = jnp.stack([hyper, down[0], down2, down[1]])
        up_a, down_a = along_y(here_a, 1), along_y(here_a, -1)
        here_b = jnp.stack([across, up[1], up2, up[0]])
        up_b, down_b = along_y(here_b, 1), along_y(here_b, -1)
        total = backward((0,), None, None, applied == 1, tables, inc0, inc1, ((here_a, here_b),))
        up_a, down_b, total = lax.optimization_barrier((up_a, down_b, total))
        far_a, far_b = along_y(up_a, 1), along_y(down_b, -1)
        total = backward(
            (3, 1),
            total,
            None,
            applied == 1,
            tables,
            inc0,
            inc1,
            ((up_a, up_b), (down_a, down_b)),
        )
        if applied == 0:
            outs = [(blocks, BF)] * 2
        else:
            outs = [(2 * per, F32)] + [(per, BF)] * (2 * (NX - 1))
        parts = backward((2,), total, outs, applied == 1, tables, inc0, inc1, ((far_a, far_b),))
        if applied == 0:
            p, q = parts
            up_p, down_q = along_x(p, 1), along_x(q, -1)
            up_q, down_p = along_x(q, 1), along_x(p, -1)
            far_p, far_q = along_x(up_p, 1), along_x(down_q, -1)
            st = tuple(
                (over(r) * (over(r) * sum(n.astype(F32) for n in group))).astype(BF)
                for r, group in zip(scale, ((p, up_p, down_p, far_p), (q, up_q, down_q, far_q)))
            )
    own, p1, q1, p2, q2, p3, q3 = parts
    p2, q2 = along_x(p2, 1), along_x(q2, -1)
    up = along_x(jnp.concatenate([plus(p1, p2), q1]), 1).astype(F32)
    down = along_x(jnp.concatenate([p3, plus(q3, q2)]), -1).astype(F32)
    current = own_scale * (own + up + down)
    kept, came = current[:per], to_sibling(current[per:])
    pair = jnp.stack([jnp.where(first, kept, came), jnp.where(first, came, kept)])
    return pair.transpose(1, 3, 0, 2).reshape(per * T, NC * T)


def solution(mesh):
    placed = (
        P("vert", None),
        P("vert", None, "edge"),
        P("vert", "edge"),
        P("vert", "edge"),
        P("vert", "edge"),
        P("vert", "edge"),
        P("vert", "edge"),
        P("vert"),
    )
    return jax.shard_map(
        shards, mesh=mesh, in_specs=placed, out_specs=P(("vert", "edge"), None), check_vma=False
    )
```
